32 devices in a mesh: section: 2 (over y), dp: 16 (over z, x, core).
Axes of the slice: x: 2, y: 2, z: 4, core: 2. Of those that a mesh axis runs over, the one named last changes fastest.
Arguments:
- queries: bfloat16 [2, 16, 256, 2560], P('section', 'dp'), may hold values from -32 to 32
- keys: bfloat16 [16, 256, 512], P('dp', 'section'), may hold values from -12 to 12
- values: bfloat16 [16, 256, 512], P('dp', 'section'), may hold values from -6 to 6
- query_gain: float32 [2, 2560], P('section'), may hold values from 0.5 to 1.5
- key_channel_scale: float32 [2, 512], P('section'), may hold values from 0.5 to 1.5
- out_grad: bfloat16 [2, 16, 256, 2560], P('section', 'dp'), may hold values from -110 to 110
- doc_start: int32 [16], P('dp'), may hold values from 1 to 255
Outputs:
- query_grad: bfloat16 [2, 16, 256, 2560], P('section', 'dp')
- key_grad: bfloat16 [16, 256, 512], P('dp', 'section')
- value_grad: bfloat16 [16, 256, 512], P('dp', 'section')
- query_gain_grad: float32 [2, 2560], P('section')
- key_gain_grad: float32 [2, 512], P('section')
The draws below stay inside these ranges and needn't reach their ends.
All inputs are finite; a program needn't handle non-finite values.
Results may differ from the reference program's by a relative error of at most 0.012.
The reference program's roundings to bfloat16 on the way (of `scaled_q`, `scaled_k`, `prob_low` and `d_score`) count: a program that leaves them out, or rounds other values in their place, can miss the bound.
Values may be sent and summed in bfloat16 or wider, within the bound.
A program may use at most 64 MiB of HBM per device.

```python
import jax
import jax.numpy as jnp
from jax import lax

QUERY_HEADS = 20
KEY_VALUE_HEADS = 4
HEAD_SIZE = 128
SEQUENCE_LENGTH = 256
DECODER_LAYERS = 2
BATCH_SEQUENCES = 16


def paired_draw(key):
    base_key = jax.random.fold_in(key, 1234)
    first_key_block, key_b = jax.random.split(base_key, 2)
    sampled_keys = jnp.clip(jax.random.normal(first_key_block, (BATCH_SEQUENCES, SEQUENCE_LENGTH, KEY_VALUE_HEADS * HEAD_SIZE), jnp.float32), -4.0, 4.0)
    queries_drawn = jnp.clip(jax.random.normal(key_b, (DECODER_LAYERS, BATCH_SEQUENCES, SEQUENCE_LENGTH, QUERY_HEADS * HEAD_SIZE), jnp.float32), -4.0, 4.0)
    return (sampled_keys, queries_drawn)


def draw_keys(key, part):
    return paired_draw(key)[0].astype(jnp.bfloat16)


def draw_queries(key, part):
    return paired_draw(key)[1].astype(jnp.bfloat16)


def draw_out_grad(key, part):
    base_key = jax.random.fold_in(key, 5678)
    first_key_block, key_b, key_c = jax.random.split(base_key, 3)
    shape_full = (DECODER_LAYERS, BATCH_SEQUENCES, SEQUENCE_LENGTH, QUERY_HEADS * HEAD_SIZE)
    row_scale = jnp.exp(jax.random.uniform(key_b, (DECODER_LAYERS, BATCH_SEQUENCES, SEQUENCE_LENGTH, 1), jnp.float32) * jnp.log(10.0))
    col_scale = jnp.exp(jax.random.uniform(key_c, (1, 1, 1, QUERY_HEADS * HEAD_SIZE), jnp.float32) * jnp.log(10.0))
    ramp = jnp.arange(BATCH_SEQUENCES).astype(jnp.float32) / max(BATCH_SEQUENCES - 1, 1)
    rising = (1.0 + 2.0 * ramp).reshape(1, BATCH_SEQUENCES, 1, 1)
    noise = jnp.clip(jax.random.normal(first_key_block, shape_full, jnp.float32), -4.0, 4.0)
    return (0.03 * noise * row_scale * col_scale * rising).astype(jnp.bfloat16)


def plant(values, rng, low, top_value):
    longest = values.shape.index(max(values.shape))
    spots = []
    for shift in (0, 1):
        where = [jax.random.randint(jax.random.fold_in(rng, axis), (), 0, length) for axis, length in enumerate(values.shape)]
        where[longest] = (where[longest] + shift) % values.shape[longest]
        spots.append(tuple(where))
    return values.at[spots[0]].set(low).at[spots[1]].set(top_value)


def block_scale(rng, shape, cuts, low, high):
    loudness = 1.0
    for position, shards_of in cuts:
        heights = jax.random.uniform(jax.random.fold_in(jax.random.fold_in(rng, 6), position), (shards_of,), jnp.float32, low / len(cuts), high / len(cuts))
        loudness = loudness * jnp.repeat(jnp.exp(heights), shape[position] // shards_of).reshape((-1,) + (1,) * (len(shape) - 1 - position))
    return loudness


def bell_draw(own_key, shape, scale, bound, pieces=(), dtype=jnp.bfloat16):
    factor_of = block_scale(own_key, shape, pieces, -0.22, 0.18) if pieces else 1.0
    values = jax.random.normal(own_key, shape, jnp.float32) * scale * factor_of
    return jnp.minimum(jnp.maximum(values, -bound), bound).astype(dtype)


def setup_inputs(seed: int = 0) -> dict:
    key_list = jax.random.split(jax.random.key(seed), 8)
    queries = draw_queries(jax.random.fold_in(key_list[7], 71), 0)
    keys = draw_keys(jax.random.fold_in(key_list[7], 71), 0)
    values = bell_draw(key_list[2], (BATCH_SEQUENCES, SEQUENCE_LENGTH, KEY_VALUE_HEADS * HEAD_SIZE), 1.0, 6.0, ((0, 16), (1, 2)))
    query_gain = jnp.clip(1.0 + 0.1 * jax.random.normal(key_list[3], (DECODER_LAYERS, QUERY_HEADS * HEAD_SIZE), jnp.float32), 0.5, 1.5)
    key_channel_scale = jnp.clip(1.0 + 0.1 * jax.random.normal(key_list[4], (DECODER_LAYERS, KEY_VALUE_HEADS * HEAD_SIZE), jnp.float32), 0.5, 1.5)
    out_grad = draw_out_grad(jax.random.fold_in(key_list[7], 71), 0)
    doc_start = plant(jax.random.randint(key_list[6], (BATCH_SEQUENCES,), 1, SEQUENCE_LENGTH), jax.random.fold_in(key_list[6], 1), 1, SEQUENCE_LENGTH - 1).astype(jnp.int32)
    return dict(queries=queries, keys=keys, values=values, query_gain=query_gain, key_channel_scale=key_channel_scale, out_grad=out_grad, doc_start=doc_start)


def sequence_grads(query_rows, key_rows, value_rows, dout_rows, q_scale, k_scale, doc_first):
    length = query_rows.shape[0]
    kv_width = key_rows.shape[1]
    heads_kv = kv_width // HEAD_SIZE
    heads_per_group = query_rows.shape[1] // kv_width
    score_scale = HEAD_SIZE ** -0.5
    scaled_q = (query_rows.astype(jnp.float32) * q_scale).astype(jnp.bfloat16)
    scaled_k = (key_rows.astype(jnp.float32) * k_scale).astype(jnp.bfloat16)
    q_heads = scaled_q.astype(jnp.float32).reshape(length, heads_kv, heads_per_group, HEAD_SIZE)
    k_heads = scaled_k.astype(jnp.float32).reshape(length, heads_kv, HEAD_SIZE)
    val_heads = value_rows.astype(jnp.float32).reshape(length, heads_kv, HEAD_SIZE)
    grad_out = dout_rows.astype(jnp.float32).reshape(length, heads_kv, heads_per_group, HEAD_SIZE)
    logits = jnp.einsum("igrd,jgd->grij", q_heads, k_heads) * score_scale
    row_pos = lax.broadcasted_iota(jnp.int32, (length, length), 0)
    col_pos = lax.broadcasted_iota(jnp.int32, (length, length), 1)
    visible = (col_pos <= row_pos) & ((row_pos < doc_first) | (col_pos >= doc_first))
    masked = jnp.where(visible, logits, -1e30)
    row_max = jnp.max(masked, axis=-1, keepdims=True)
    expo = jnp.where(visible, jnp.exp(masked - row_max), 0.0)
    attn_prob = expo / jnp.sum(expo, axis=-1, keepdims=True)
    prob_low = attn_prob.astype(jnp.bfloat16).astype(jnp.float32)
    value_term = jnp.einsum("grij,igrd->jgd", prob_low, grad_out).reshape(length, kv_width)
    d_prob = jnp.einsum("igrd,jgd->grij", grad_out, val_heads)
    row_delta = jnp.sum(attn_prob * d_prob, axis=-1, keepdims=True)
    d_score = (attn_prob * (d_prob - row_delta) * score_scale).astype(jnp.bfloat16).astype(jnp.float32)
    dq_scaled = jnp.einsum("grij,jgd->igrd", d_score, k_heads).reshape(length, -1)
    dk_scaled = jnp.einsum("grij,igrd->jgd", d_score, q_heads).reshape(length, kv_width)
    query_grad = (dq_scaled * q_scale).astype(jnp.bfloat16)
    key_term = dk_scaled * k_scale
    q_gain_term = jnp.sum(dq_scaled * query_rows.astype(jnp.float32), axis=0)
    k_gain_term = jnp.sum(dk_scaled * key_rows.astype(jnp.float32), axis=0)
    return query_grad, key_term, value_term, q_gain_term, k_gain_term


def reference(queries, keys, values, query_gain, key_channel_scale, out_grad, doc_start):
    def one_section(carry, section_in):
        section_q, section_dout, q_scale, k_scale = section_in

        def one_sequence(items):
            query_rows, key_rows, value_rows, dout_rows, doc_first = items
            return sequence_grads(query_rows, key_rows, value_rows, dout_rows, q_scale, k_scale, doc_first)

        query_grad, key_term, value_term, q_terms, k_terms = lax.map(one_sequence, (section_q, keys, values, section_dout, doc_start))
        key_acc, value_acc = carry
        return (key_acc + key_term, value_acc + value_term), (query_grad, jnp.sum(q_terms, axis=0) / BATCH_SEQUENCES, jnp.sum(k_terms, axis=0) / BATCH_SEQUENCES)

    start_acc = (jnp.zeros(keys.shape, jnp.float32), jnp.zeros(values.shape, jnp.float32))
    (key_acc, value_acc), (query_grad, query_gain_grad, key_gain_grad) = lax.scan(one_section, start_acc, (queries, out_grad, query_gain, key_channel_scale))
    return query_grad, key_acc.astype(jnp.bfloat16), value_acc.astype(jnp.bfloat16), query_gain_grad, key_gain_grad
```

```python
import functools
import math

import jax
import jax.numpy as jnp
from jax import lax
from jax.experimental import pallas as pl
from jax.experimental.pallas import tpu as pltpu
from jax.sharding import PartitionSpec as P

HEAD = 128
LAG = 2
DIRECT = 16
NEAR = 4
MESH = pl.DeviceIdType.MESH
BF = jnp.bfloat16
F32 = jnp.float32
NT = (((1,), (1,)), ((), ()))


def radices(n):
    out = []
    while n > 1:
        r = next((r for r in range(DIRECT, 1, -1) if n % r == 0), n)
        out.append(r)
        n //= r
    return out


def near_split(stages):
    if len(stages) == 1 and stages[0] % NEAR == 0:
        return NEAR, stages[0] // NEAR
    return 0, 0


def kernel(
    sections, replicas, stages,
    doc_hbm, q_hbm, k_hbm, v_hbm, qs_hbm, ks_hbm, do_hbm,
    dq_ref, kg_ref, vg_ref, qgain_ref, kgain_ref,
    doc_ref, qs_ref, ks_ref, q_vm, do_vm, k_vm, v_vm, bias, grad, gsend, grecv, *rest,
):
    n_st = len(stages)
    slots = rest[:n_st]
    (small_sem, q_sem, do_sem, kl_sem, vl_sem, kv_ss, kv_rs, g_ss, g_rs) = rest[n_st:n_st + 9]
    st_ss = rest[n_st + 9:2 * n_st + 9]
    st_rs = rest[2 * n_st + 9:3 * n_st + 9]
    line_sems = rest[3 * n_st + 9:]
    groups, length, width = q_vm.shape
    per = width // HEAD
    rows = k_hbm.shape[1]
    half = length // 2
    scale = HEAD ** -0.5
    to_exp2 = scale * math.log2(math.e)
    sec = lax.axis_index("section")
    dp = lax.axis_index("dp")

    def sec_peer(off):
        return lax.rem(sec + off, sections)

    strides = []
    stride = 1
    for r in stages:
        strides.append(stride)
        stride *= r

    def member(s):
        return lax.rem(dp // strides[s], stages[s])

    def st_peer(s, off):
        mine = member(s)
        other = lax.rem(mine + off, stages[s])
        return dp + (other - mine) * strides[s]

    near, far = near_split(stages)
    row = dp // near if near else 0

    def line_signal(sem):
        @pl.when(row > 0)
        def _():
            pl.semaphore_signal(sem, inc=1, device_id={"dp": dp - near}, device_id_type=MESH)

        @pl.when(row < far - 1)
        def _():
            pl.semaphore_signal(sem, inc=1, device_id={"dp": dp + near}, device_id_type=MESH)

    line_count = jnp.where(row > 0, 1, 0) + jnp.where(row < far - 1, 1, 0)
    barrier = pltpu.get_barrier_semaphore()
    count = 0
    for off in range(1, sections):
        pl.semaphore_signal(barrier, inc=1, device_id={"section": sec_peer(off)}, device_id_type=MESH)
        count += 1
    if near:
        for off in range(1, near):
            other = row * near + lax.rem(lax.rem(dp, near) + off, near)
            pl.semaphore_signal(barrier, inc=1, device_id={"dp": other}, device_id_type=MESH)
            count += 1
        if far > 1:
            line_signal(barrier)
            count = count + line_count
    else:
        for s in range(n_st):
            for off in range(1, stages[s]):
                pl.semaphore_signal(barrier, inc=1, device_id={"dp": st_peer(s, off)}, device_id_type=MESH)
                count += 1

    my_rows = pl.ds(pl.multiple_of(sec * rows, rows), rows)

    def hcols(g):
        return pl.ds(pl.multiple_of(g * HEAD, HEAD), HEAD)

    def wcols(g):
        return pl.ds(pl.multiple_of(g * width, HEAD), width)

    def local_in(g):
        return (
            pltpu.make_async_copy(k_hbm.at[0, :, hcols(g)], k_vm.at[g, my_rows, :], kl_sem.at[g]),
            pltpu.make_async_copy(v_hbm.at[0, :, hcols(g)], v_vm.at[g, my_rows, :], vl_sem.at[g]),
            pltpu.make_async_copy(q_hbm.at[0, 0, :, wcols(g)], q_vm.at[g], q_sem.at[g]),
            pltpu.make_async_copy(do_hbm.at[0, 0, :, wcols(g)], do_vm.at[g], do_sem.at[g]),
        )

    def kv_copies(g, off):
        made = []
        for src, dst in ((k_hbm, k_vm), (v_hbm, v_vm)):
            made.append(pltpu.make_async_remote_copy(
                src_ref=src.at[0, :, hcols(g)],
                dst_ref=dst.at[g, my_rows, :],
                send_sem=kv_ss.at[off - 1],
                recv_sem=kv_rs.at[off - 1, g],
                device_id={"section": sec_peer(off)},
                device_id_type=MESH,
            ))
        return made

    def grad_copy(g, off):
        peer = sec_peer(off)
        return pltpu.make_async_remote_copy(
            src_ref=gsend.at[g, pl.ds(pl.multiple_of(peer * rows, rows), rows), :],
            dst_ref=grecv.at[off - 1, g],
            send_sem=g_ss.at[off - 1],
            recv_sem=g_rs.at[off - 1, g],
            device_id={"section": peer},
            device_id_type=MESH,
        )

    def st_copy(s, g, off):
        mine = member(s)
        return pltpu.make_async_remote_copy(
            src_ref=slots[s].at[g, mine],
            dst_ref=slots[s].at[g, mine],
            send_sem=st_ss[s],
            recv_sem=st_rs[s].at[g],
            device_id={"dp": st_peer(s, off)},
            device_id_type=MESH,
        )

    def drain(ref, sem):
        pltpu.make_async_copy(ref, ref, sem).wait()

    def st_total(s, g):
        drain(slots[s].at[g, :stages[s] - 1], st_rs[s].at[g])
        total = slots[s][g, 0]
        for m in range(1, stages[s]):
            total = total + slots[s][g, m]
        return total

    def st_start(s, g):
        for off in range(1, stages[s]):
            st_copy(s, g, off).start()

    def st_send(s, g, value):
        slots[s][g, member(s)] = value
        st_start(s, g)

    small = [
        pltpu.make_async_copy(src, dst, small_sem.at[i])
        for i, (src, dst) in enumerate(((doc_hbm, doc_ref), (qs_hbm, qs_ref), (ks_hbm, ks_ref)))
    ]
    for c in small:
        c.start()

    @pl.loop(0, groups)
    def _(g):
        for c in local_in(g):
            c.start()

    pl.semaphore_wait(barrier, count)

    @pl.loop(0, groups)
    def _(g):
        for off in range(1, sections):
            for c in kv_copies(g, off):
                c.start()

    if line_sems:
        line_signal(line_sems[0])

    for c in small:
        c.wait()
    doc = doc_ref[0]
    j_pos = lax.broadcasted_iota(jnp.int32, (length, length), 0)
    i_pos = lax.broadcasted_iota(jnp.int32, (length, length), 1)
    visible = (j_pos <= i_pos) & ((i_pos < doc) | (j_pos >= doc))
    bias[...] = jnp.where(visible, 0.0, -1e30).astype(F32)

    def one_group(g, carry):
        for c in local_in(g):
            c.wait()
        for off in range(1, sections):
            drain(grecv.at[off - 1, g], kv_rs.at[off - 1, g])
        k_scale = ks_ref[:, hcols(g)]
        k_raw = k_vm[g].astype(F32)
        k_f = k_raw * k_scale
        k_low = k_f.astype(BF)
        k_t = k_low.astype(F32).T.astype(BF)
        val = v_vm[g]
        k0, k1 = k_low[:half], k_low[half:]
        v0, v1 = val[:half], val[half:]
        sums = [None] * 4
        gain_rows = []

        def scores(h):
            cols = slice(h * HEAD, (h + 1) * HEAD)
            q_scale = qs_ref[:, pl.ds(pl.multiple_of(g * width + h * HEAD, HEAD), HEAD)]
            q_low = (q_vm[g, :, cols].astype(F32) * q_scale).astype(BF)
            d_out = do_vm[g, :, cols]
            s0 = lax.dot_general(k0, q_low, NT, preferred_element_type=F32)
            s1 = lax.dot_general(k1, q_low[half:], NT, preferred_element_type=F32)
            d0 = lax.dot_general(v0, d_out, NT, preferred_element_type=F32)
            d1 = lax.dot_general(v1, d_out[half:], NT, preferred_element_type=F32)
            return q_low, s0, s1, d0, d1

        def softmax(s0, s1, d0, d1):
            s0 = s0 + bias[:half, :]
            s1 = s1 + bias[half:, half:]
            m0 = jnp.max(s0, axis=0, keepdims=True)
            m1 = jnp.max(s1, axis=0, keepdims=True)
            m_b = jnp.maximum(m0[:, half:], m1)
            m0 = jnp.concatenate([m0[:, :half], m_b], axis=1)
            e0 = jnp.exp2((s0 - m0) * to_exp2)
            e1 = jnp.exp2((s1 - m_b) * to_exp2)
            t0 = jnp.sum(e0, axis=0, keepdims=True)
            t1 = jnp.sum(e1, axis=0, keepdims=True)
            t0 = jnp.concatenate([t0[:, :half], t0[:, half:] + t1], axis=1)
            inv = 1.0 / t0
            p0 = e0 * inv
            p1 = e1 * inv[:, half:]
            r0 = jnp.sum(p0 * d0, axis=0, keepdims=True)
            r1 = jnp.sum(p1 * d1, axis=0, keepdims=True)
            r0 = jnp.concatenate([r0[:, :half], r0[:, half:] + r1], axis=1)
            ds0 = (p0 * (d0 - r0) * scale).astype(BF)
            ds1 = (p1 * (d1 - r0[:, half:]) * scale).astype(BF)
            return p0.astype(BF), p1.astype(BF), ds0, ds1

        def grads(h, q_low, p0_low, p1_low, ds0, ds1):
            cols = slice(h * HEAD, (h + 1) * HEAD)
            q_scale = qs_ref[:, pl.ds(pl.multiple_of(g * width + h * HEAD, HEAD), HEAD)]
            d_out = do_vm[g, :, cols]
            made = (
                jnp.dot(p0_low, d_out, preferred_element_type=F32),
                jnp.dot(p1_low, d_out[half:], preferred_element_type=F32),
                jnp.dot(ds0, q_low, preferred_element_type=F32),
                jnp.dot(ds1, q_low[half:], preferred_element_type=F32),
            )
            for i, x in enumerate(made):
                sums[i] = x if h == 0 else sums[i] + x
            ds_full = jnp.concatenate(
                [ds0, jnp.concatenate([jnp.zeros((half, half), BF), ds1], axis=1)], axis=0
            )
            dq = jnp.dot(k_t, ds_full, preferred_element_type=F32).T
            dq_ref[0, 0, :, pl.ds(pl.multiple_of(g * width + h * HEAD, HEAD), HEAD)] = (dq * q_scale).astype(BF)
            gain_rows.append(jnp.sum(dq * q_vm[g, :, cols].astype(F32), axis=0, keepdims=True))

        ahead = scores(0)
        for h in range(per):
            q_low, *sd = ahead
            if h + 1 < per:
                ahead = scores(h + 1)
            grads(h, q_low, *softmax(*sd))
        dv0, dv1, dk0, dk1 = sums
        dk = jnp.concatenate([dk0, dk1], axis=0)
        dv = jnp.concatenate([dv0, dv1], axis=0)
        key_term = dk * k_scale
        grad[g, :, :HEAD] = key_term
        grad[g, :, HEAD:] = dv
        gsend[g, :, :HEAD] = key_term.astype(BF)
        gsend[g, :, HEAD:] = dv.astype(BF)
        for off in range(1, sections):
            grad_copy(g, off).start()
        gain_rows.append(jnp.sum(dk * k_raw, axis=0, keepdims=True))
        spare = slots[0].shape[2] - len(gain_rows)
        if spare:
            gain_rows.append(jnp.zeros((spare, HEAD), F32))
        gain_block = jnp.concatenate(gain_rows, axis=0)
        slots[0][g, member(0)] = gain_block
        for i in range(len(line_sems)):
            @pl.when(g == i)
            def _():
                pl.semaphore_wait(line_sems[i], line_count)
                if i + 1 < len(line_sems):
                    line_signal(line_sems[i + 1])
        hold = max(len(line_sems) - 1, 0)

        @pl.when(g == hold)
        def _():
            for e in range(hold):
                st_start(0, e)

        @pl.when(g >= hold)
        def _():
            st_start(0, g)

        for s in range(1, n_st):
            @pl.when(g >= LAG * s)
            def _():
                st_send(s, g - LAG * s, st_total(s - 1, g - LAG * s))
        return carry

    lax.fori_loop(0, groups, one_group, 0)

    def finish_gain(g):
        total = st_total(n_st - 1, g) * (1.0 / replicas)
        for h in range(per):
            qgain_ref[:, (g * per + h) * HEAD:(g * per + h + 1) * HEAD] = total[h:h + 1]
        kgain_ref[:, g * HEAD:(g + 1) * HEAD] = total[per:per + 1]

    def finish_grad(g):
        total = grad[g, my_rows, :]
        for off in range(1, sections):
            grad_copy(g, off).wait_recv()
            total = total + grecv[off - 1, g].astype(F32)
        kg_ref[0, :, g * HEAD:(g + 1) * HEAD] = total[:, :HEAD].astype(BF)
        vg_ref[0, :, g * HEAD:(g + 1) * HEAD] = total[:, HEAD:].astype(BF)

    for t in range(groups, groups + LAG * (n_st - 1)):
        for s in range(n_st - 1, 0, -1):
            g = t - LAG * s
            if 0 <= g < groups:
                st_send(s, g, st_total(s - 1, g))
    for g in range(groups):
        finish_grad(g)
    for g in range(groups):
        finish_gain(g)

    for off in range(1, sections):
        drain(grecv.at[off - 1], kv_ss.at[off - 1])
        drain(grecv.at[off - 1], g_ss.at[off - 1])
    for s in range(n_st):
        drain(slots[s].at[:, :stages[s] - 1], st_ss[s])


def write_out(*refs):
    n = len(refs) // 2
    sems = refs[-1]
    copies = [pltpu.make_async_copy(refs[i], refs[n + i], sems.at[i]) for i in range(n)]
    for c in copies:
        c.start()
    for c in copies:
        c.wait()


def solution(mesh):
    sections = mesh.shape["section"]
    replicas = mesh.shape["dp"]
    stages = radices(replicas)
    n_st = len(stages)

    def on_device(queries, keys, values, query_gain, key_channel_scale, out_grad, doc_start):
        length = queries.shape[2]
        rows, kv_width = keys.shape[1], keys.shape[2]
        groups = kv_width // HEAD
        width = queries.shape[3] // groups
        gain_rows = -(-(width // HEAD + 1) // 8) * 8
        vmem = pl.BlockSpec(memory_space=pltpu.VMEM)
        hbm = pl.BlockSpec(memory_space=pl.ANY)
        dma = pltpu.SemaphoreType.DMA
        peers = sections - 1
        scratch = [
            pltpu.SMEM(doc_start.shape, jnp.int32),
            pltpu.VMEM(query_gain.shape, F32),
            pltpu.VMEM(key_channel_scale.shape, F32),
            pltpu.VMEM((groups, length, width), BF),
            pltpu.VMEM((groups, length, width), BF),
            pltpu.VMEM((groups, length, HEAD), BF),
            pltpu.VMEM((groups, length, HEAD), BF),
            pltpu.VMEM((length, length), F32),
            pltpu.VMEM((groups, length, 2 * HEAD), F32),
            pltpu.VMEM((groups, length, 2 * HEAD), BF),
            pltpu.VMEM((peers, groups, rows, 2 * HEAD), BF),
        ]
        scratch += [pltpu.VMEM((groups, r, gain_rows, HEAD), F32) for r in stages]
        scratch += [dma((3,))] + [dma((groups,))] * 4
        scratch += [dma((peers,)), dma((peers, groups))] * 2
        scratch += [dma] * n_st + [dma((groups,))] * n_st
        scratch += [pltpu.SemaphoreType.REGULAR] * max(near_split(stages)[1] - 1, 0)
        shapes = (
            jax.ShapeDtypeStruct(queries.shape, BF),
            jax.ShapeDtypeStruct(keys.shape, BF),
            jax.ShapeDtypeStruct(values.shape, BF),
            jax.ShapeDtypeStruct(query_gain.shape, F32),
            jax.ShapeDtypeStruct(key_channel_scale.shape, F32),
        )
        held = pl.pallas_call(
            functools.partial(kernel, sections, replicas, stages),
            out_shape=tuple(pltpu.VMEM(x.shape, x.dtype) for x in shapes),
            in_specs=[pl.BlockSpec(memory_space=pltpu.HBM)] + [hbm] * 6,
            out_specs=(vmem,) * 5,
            scratch_shapes=scratch,
            compiler_params=pltpu.CompilerParams(collective_id=0, has_side_effects=True),
        )(doc_start, queries, keys, values, query_gain, key_channel_scale, out_grad)
        return pl.pallas_call(
            write_out,
            out_shape=shapes,
            in_specs=[vmem] * 5,
            out_specs=(hbm,) * 5,
            scratch_shapes=[dma((5,))],
        )(*[pltpu.with_memory_space_constraint(x, pltpu.VMEM) for x in held])

    in_specs = (
        P("section", "dp", None, None),
        P("dp", "section", None),
        P("dp", "section", None),
        P("section", None),
        P("section", None),
        P("section", "dp", None, None),
        P("dp"),
    )
    out_specs = (
        P("section", "dp", None, None),
        P("dp", "section", None),
        P("dp", "section", None),
        P("section", None),
        P("section", None),
    )
    return jax.shard_map(
        on_device, mesh=mesh, in_specs=in_specs, out_specs=out_specs, check_vma=False
    )
```

```python
import functools
import math

import jax
import jax.numpy as jnp
from jax import lax
from jax.experimental import pallas as pl
from jax.experimental.pallas import tpu as pltpu
from jax.sharding import PartitionSpec as P

HEAD = 128
LAG = 2
DIRECT = 16
NEAR = 4
MESH = pl.DeviceIdType.MESH
BF = jnp.bfloat16
F32 = jnp.float32
NT = (((1,), (1,)), ((), ()))


def radices(n):
    out = []
    while n > 1:
        r = next((r for r in range(DIRECT, 1, -1) if n % r == 0), n)
        out.append(r)
        n //= r
    return out


def near_split(stages):
    if len(stages) == 1 and stages[0] % NEAR == 0:
        return NEAR, stages[0] // NEAR
    return 0, 0


def kernel(
    sections, replicas, stages,
    doc_hbm, q_hbm, k_hbm, v_hbm, qs_hbm, ks_hbm, do_hbm,
    dq_ref, kg_ref, vg_ref, qgain_ref, kgain_ref,
    doc_ref, qs_ref, ks_ref, q_vm, do_vm, k_vm, v_vm, ql_vm, qf_vm, sbuf, dbuf, pbuf, dsbuf, bias, grad, gsend, grecv, *rest,
):
    n_st = len(stages)
    slots = rest[:n_st]
    (small_sem, q_sem, do_sem, kl_sem, vl_sem, kv_ss, kv_rs, g_ss, g_rs) = rest[n_st:n_st + 9]
    st_ss = rest[n_st + 9:2 * n_st + 9]
    st_rs = rest[2 * n_st + 9:3 * n_st + 9]
    line_sems = rest[3 * n_st + 9:]
    groups, length, width = q_vm.shape
    per = width // HEAD
    rows = k_hbm.shape[1]
    half = length // 2
    scale = HEAD ** -0.5
    to_exp2 = scale * math.log2(math.e)
    sec = lax.axis_index("section")
    dp = lax.axis_index("dp")

    def sec_peer(off):
        return lax.rem(sec + off, sections)

    strides = []
    stride = 1
    for r in stages:
        strides.append(stride)
        stride *= r

    def member(s):
        return lax.rem(dp // strides[s], stages[s])

    def st_peer(s, off):
        mine = member(s)
        other = lax.rem(mine + off, stages[s])
        return dp + (other - mine) * strides[s]

    near, far = near_split(stages)
    row = dp // near if near else 0

    def line_signal(sem):
        @pl.when(row > 0)
        def _():
            pl.semaphore_signal(sem, inc=1, device_id={"dp": dp - near}, device_id_type=MESH)

        @pl.when(row < far - 1)
        def _():
            pl.semaphore_signal(sem, inc=1, device_id={"dp": dp + near}, device_id_type=MESH)

    line_count = jnp.where(row > 0, 1, 0) + jnp.where(row < far - 1, 1, 0)
    barrier = pltpu.get_barrier_semaphore()
    count = 0
    for off in range(1, sections):
        pl.semaphore_signal(barrier, inc=1, device_id={"section": sec_peer(off)}, device_id_type=MESH)
        count += 1
    if near:
        for off in range(1, near):
            other = row * near + lax.rem(lax.rem(dp, near) + off, near)
            pl.semaphore_signal(barrier, inc=1, device_id={"dp": other}, device_id_type=MESH)
            count += 1
        if far > 1:
            line_signal(barrier)
            count = count + line_count
    else:
        for s in range(n_st):
            for off in range(1, stages[s]):
                pl.semaphore_signal(barrier, inc=1, device_id={"dp": st_peer(s, off)}, device_id_type=MESH)
                count += 1

    my_rows = pl.ds(pl.multiple_of(sec * rows, rows), rows)

    def hcols(g):
        return pl.ds(pl.multiple_of(g * HEAD, HEAD), HEAD)

    def wcols(g):
        return pl.ds(pl.multiple_of(g * width, HEAD), width)

    def local_in(g):
        return (
            pltpu.make_async_copy(k_hbm.at[0, :, hcols(g)], k_vm.at[g, my_rows, :], kl_sem.at[g]),
            pltpu.make_async_copy(v_hbm.at[0, :, hcols(g)], v_vm.at[g, my_rows, :], vl_sem.at[g]),
            pltpu.make_async_copy(do_hbm.at[0, 0, :, wcols(g)], do_vm.at[g], do_sem.at[g]),
        )

    def q_in(g):
        return pltpu.make_async_copy(q_hbm.at[0, 0, :, wcols(g)], q_vm.at[g], q_sem.at[g])

    def kv_copies(g, off):
        made = []
        for src, dst in ((k_hbm, k_vm), (v_hbm, v_vm)):
            made.append(pltpu.make_async_remote_copy(
                src_ref=src.at[0, :, hcols(g)],
                dst_ref=dst.at[g, my_rows, :],
                send_sem=kv_ss.at[off - 1],
                recv_sem=kv_rs.at[off - 1, g],
                device_id={"section": sec_peer(off)},
                device_id_type=MESH,
            ))
        return made

    def grad_copy(g, off):
        peer = sec_peer(off)
        return pltpu.make_async_remote_copy(
            src_ref=gsend.at[g, pl.ds(pl.multiple_of(peer * rows, rows), rows), :],
            dst_ref=grecv.at[off - 1, g],
            send_sem=g_ss.at[off - 1],
            recv_sem=g_rs.at[off - 1, g],
            device_id={"section": peer},
            device_id_type=MESH,
        )

    def st_copy(s, g, off):
        mine = member(s)
        return pltpu.make_async_remote_copy(
            src_ref=slots[s].at[g, mine],
            dst_ref=slots[s].at[g, mine],
            send_sem=st_ss[s],
            recv_sem=st_rs[s].at[g],
            device_id={"dp": st_peer(s, off)},
            device_id_type=MESH,
        )

    def drain(ref, sem):
        pltpu.make_async_copy(ref, ref, sem).wait()

    def st_total(s, g):
        drain(slots[s].at[g, :stages[s] - 1], st_rs[s].at[g])
        total = slots[s][g, 0]
        for m in range(1, stages[s]):
            total = total + slots[s][g, m]
        return total

    def st_start(s, g):
        for off in range(1, stages[s]):
            st_copy(s, g, off).start()

    def st_send(s, g, value):
        slots[s][g, member(s)] = value
        st_start(s, g)

    small = [
        pltpu.make_async_copy(src, dst, small_sem.at[i])
        for i, (src, dst) in enumerate(((doc_hbm, doc_ref), (qs_hbm, qs_ref), (ks_hbm, ks_ref)))
    ]
    for c in small:
        c.start()

    @pl.loop(0, groups)
    def _(g):
        q_in(g).start()
        for c in local_in(g):
            c.start()

    pl.semaphore_wait(barrier, count)

    @pl.loop(0, groups)
    def _(g):
        for off in range(1, sections):
            for c in kv_copies(g, off):
                c.start()

    if line_sems:
        line_signal(line_sems[0])

    for c in small:
        c.wait()
    doc = doc_ref[0]
    j_pos = lax.broadcasted_iota(jnp.int32, (length, length), 0)
    i_pos = lax.broadcasted_iota(jnp.int32, (length, length), 1)
    visible = (j_pos <= i_pos) & ((i_pos < doc) | (j_pos >= doc))
    shade = jnp.where(visible, 0.0, -1e30).astype(F32)
    bias[0] = shade[:half, :half]
    bias[1] = shade[:half, half:]
    bias[2] = shade[half:, half:]

    @pl.loop(0, groups)
    def _(g):
        q_in(g).wait()
        for h in range(per):
            q_f = q_vm[g, :, h * HEAD:(h + 1) * HEAD].astype(F32)
            q_scale = qs_ref[:, pl.ds(pl.multiple_of(g * width + h * HEAD, HEAD), HEAD)]
            qf_vm[g, h] = q_f
            ql_vm[g, h] = (q_f * q_scale).astype(BF)

    def one_group(g, carry):
        for c in local_in(g):
            c.wait()
        for off in range(1, sections):
            drain(grecv.at[off - 1, g], kv_rs.at[off - 1, g])
        k_scale = ks_ref[:, hcols(g)]
        k_raw = k_vm[g].astype(F32)
        k_low = (k_raw * k_scale).astype(BF)
        k_t = k_low.astype(F32).T.astype(BF)
        val = v_vm[g]
        k0, k1 = k_low[:half], k_low[half:]
        v0, v1 = val[:half], val[half:]
        gain_rows = []

        def d_out_of(h):
            return do_vm[g, :, h * HEAD:(h + 1) * HEAD]

        def scores(h):
            q_low = ql_vm[g, h]
            x = lax.dot_general(k0, q_low, NT, preferred_element_type=F32)
            sbuf[h % 2, 0], sbuf[h % 2, 1] = x[:, :half], x[:, half:]
            sbuf[h % 2, 2] = lax.dot_general(k1, q_low[half:], NT, preferred_element_type=F32)

        def d_probs(h):
            d_out = d_out_of(h)
            x = lax.dot_general(v0, d_out, NT, preferred_element_type=F32)
            dbuf[h % 2, 0], dbuf[h % 2, 1] = x[:, :half], x[:, half:]
            dbuf[h % 2, 2] = lax.dot_general(v1, d_out[half:], NT, preferred_element_type=F32)

        def softmax(h, blocks):
            b = h % 2
            xs = [sbuf[b, i] + bias[i] for i in blocks]
            top = functools.reduce(jnp.maximum, xs)
            top = jnp.max(top, axis=0, keepdims=True)
            es = [jnp.exp2((x - top) * to_exp2) for x in xs]
            inv = 1.0 / jnp.sum(functools.reduce(jnp.add, es), axis=0, keepdims=True)
            ps = [e * inv for e in es]
            r = [p * dbuf[b, i] for p, i in zip(ps, blocks)]
            r = jnp.sum(functools.reduce(jnp.add, r), axis=0, keepdims=True)
            for p, i in zip(ps, blocks):
                pbuf[b, i] = p.astype(BF)
                dsbuf[b, i] = (p * (dbuf[b, i] - r)).astype(BF)

        def wide(ref, h):
            return jnp.concatenate([ref[h % 2, 0], ref[h % 2, 1]], axis=1)

        def add(h, rows_, cols_, x):
            if h == 0:
                grad[g, rows_, cols_] = x
            else:
                grad[g, rows_, cols_] += x

        lo, hi = slice(0, half), slice(half, 2 * half)
        kc, vc = slice(0, HEAD), slice(HEAD, 2 * HEAD)

        def kv_grads(h):
            d_out, q_low = d_out_of(h), ql_vm[g, h]
            add(h, lo, vc, jnp.dot(wide(pbuf, h), d_out, preferred_element_type=F32))
            add(h, hi, vc, jnp.dot(pbuf[h % 2, 2], d_out[half:], preferred_element_type=F32))
            add(h, lo, kc, jnp.dot(wide(dsbuf, h), q_low, preferred_element_type=F32))
            add(h, hi, kc, jnp.dot(dsbuf[h % 2, 2], q_low[half:], preferred_element_type=F32))

        def q_grads(h):
            ds_full = jnp.concatenate(
                [wide(dsbuf, h), jnp.concatenate([jnp.zeros((half, half), BF), dsbuf[h % 2, 2]], axis=1)], axis=0
            )
            cols = pl.ds(pl.multiple_of(g * width + h * HEAD, HEAD), HEAD)
            dq = jnp.dot(k_t, ds_full, preferred_element_type=F32).T
            dq_ref[0, 0, :, cols] = (dq * (qs_ref[:, cols] * scale)).astype(BF)
            gain_rows.append(jnp.sum(dq * qf_vm[g, h], axis=0, keepdims=True))

        scores(0)
        d_probs(0)
        for h in range(per):
            if h + 1 < per:
                scores(h + 1)
            softmax(h, (0,))
            if h + 1 < per:
                d_probs(h + 1)
            if h:
                kv_grads(h - 1)
            softmax(h, (1, 2))
            if h:
                q_grads(h - 1)
        kv_grads(per - 1)
        q_grads(per - 1)
        dk = grad[g, :, :HEAD]
        key_term = dk * (k_scale * scale)
        grad[g, :, :HEAD] = key_term
        gsend[g, :, :HEAD] = key_term.astype(BF)
        gsend[g, :, HEAD:] = grad[g, :, HEAD:].astype(BF)
        for off in range(1, sections):
            grad_copy(g, off).start()
        gain_rows.append(jnp.sum(dk * k_raw, axis=0, keepdims=True))
        spare = slots[0].shape[2] - len(gain_rows)
        if spare:
            gain_rows.append(jnp.zeros((spare, HEAD), F32))
        gain_block = jnp.concatenate(gain_rows, axis=0)
        slots[0][g, member(0)] = gain_block
        for i in range(len(line_sems)):
            @pl.when(g == i)
            def _():
                pl.semaphore_wait(line_sems[i], line_count)
                if i + 1 < len(line_sems):
                    line_signal(line_sems[i + 1])
        hold = max(len(line_sems) - 1, 0)

        @pl.when(g == hold)
        def _():
            for e in range(hold):
                st_start(0, e)

        @pl.when(g >= hold)
        def _():
            st_start(0, g)

        for s in range(1, n_st):
            @pl.when(g >= LAG * s)
            def _():
                st_send(s, g - LAG * s, st_total(s - 1, g - LAG * s))
        return carry

    lax.fori_loop(0, groups, one_group, 0)

    def finish_gain(g):
        total = st_total(n_st - 1, g) * (scale / replicas)
        for h in range(per):
            qgain_ref[:, (g * per + h) * HEAD:(g * per + h + 1) * HEAD] = total[h:h + 1]
        kgain_ref[:, g * HEAD:(g + 1) * HEAD] = total[per:per + 1]

    def finish_grad(g):
        total = grad[g, my_rows, :]
        for off in range(1, sections):
            grad_copy(g, off).wait_recv()
            total = total + grecv[off - 1, g].astype(F32)
        kg_ref[0, :, g * HEAD:(g + 1) * HEAD] = total[:, :HEAD].astype(BF)
        vg_ref[0, :, g * HEAD:(g + 1) * HEAD] = total[:, HEAD:].astype(BF)

    for t in range(groups, groups + LAG * (n_st - 1)):
        for s in range(n_st - 1, 0, -1):
            g = t - LAG * s
            if 0 <= g < groups:
                st_send(s, g, st_total(s - 1, g))
    for g in range(groups):
        finish_grad(g)
    for g in range(groups):
        finish_gain(g)

    for off in range(1, sections):
        drain(grecv.at[off - 1], kv_ss.at[off - 1])
        drain(grecv.at[off - 1], g_ss.at[off - 1])
    for s in range(n_st):
        drain(slots[s].at[:, :stages[s] - 1], st_ss[s])


def write_out(*refs):
    n = len(refs) // 2
    sems = refs[-1]
    copies = [pltpu.make_async_copy(refs[i], refs[n + i], sems.at[i]) for i in range(n)]
    for c in copies:
        c.start()
    for c in copies:
        c.wait()


def solution(mesh):
    sections = mesh.shape["section"]
    replicas = mesh.shape["dp"]
    stages = radices(replicas)
    n_st = len(stages)

    def on_device(queries, keys, values, query_gain, key_channel_scale, out_grad, doc_start):
        length = queries.shape[2]
        rows, kv_width = keys.shape[1], keys.shape[2]
        groups, half = kv_width // HEAD, length // 2
        width = queries.shape[3] // groups
        gain_rows = -(-(width // HEAD + 1) // 8) * 8
        vmem = pl.BlockSpec(memory_space=pltpu.VMEM)
        hbm = pl.BlockSpec(memory_space=pl.ANY)
        dma = pltpu.SemaphoreType.DMA
        peers = sections - 1
        scratch = [
            pltpu.SMEM(doc_start.shape, jnp.int32),
            pltpu.VMEM(query_gain.shape, F32),
            pltpu.VMEM(key_channel_scale.shape, F32),
            pltpu.VMEM((groups, length, width), BF),
            pltpu.VMEM((groups, length, width), BF),
            pltpu.VMEM((groups, length, HEAD), BF),
            pltpu.VMEM((groups, length, HEAD), BF),
            pltpu.VMEM((groups, width // HEAD, length, HEAD), BF),
            pltpu.VMEM((groups, width // HEAD, length, HEAD), F32),
            pltpu.VMEM((2, 3, half, half), F32),
            pltpu.VMEM((2, 3, half, half), F32),
            pltpu.VMEM((2, 3, half, half), BF),
            pltpu.VMEM((2, 3, half, half), BF),
            pltpu.VMEM((3, half, half), F32),
            pltpu.VMEM((groups, length, 2 * HEAD), F32),
            pltpu.VMEM((groups, length, 2 * HEAD), BF),
            pltpu.VMEM((peers, groups, rows, 2 * HEAD), BF),
        ]
        scratch += [pltpu.VMEM((groups, r, gain_rows, HEAD), F32) for r in stages]
        scratch += [dma((3,))] + [dma((groups,))] * 4
        scratch += [dma((peers,)), dma((peers, groups))] * 2
        scratch += [dma] * n_st + [dma((groups,))] * n_st
        scratch += [pltpu.SemaphoreType.REGULAR] * max(near_split(stages)[1] - 1, 0)
        shapes = (
            jax.ShapeDtypeStruct(queries.shape, BF),
            jax.ShapeDtypeStruct(keys.shape, BF),
            jax.ShapeDtypeStruct(values.shape, BF),
            jax.ShapeDtypeStruct(query_gain.shape, F32),
            jax.ShapeDtypeStruct(key_channel_scale.shape, F32),
        )
        held = pl.pallas_call(
            functools.partial(kernel, sections, replicas, stages),
            out_shape=tuple(pltpu.VMEM(x.shape, x.dtype) for x in shapes),
            in_specs=[pl.BlockSpec(memory_space=pltpu.HBM)] + [hbm] * 6,
            out_specs=(vmem,) * 5,
            scratch_shapes=scratch,
            compiler_params=pltpu.CompilerParams(collective_id=0, has_side_effects=True),
        )(doc_start, queries, keys, values, query_gain, key_channel_scale, out_grad)
        return pl.pallas_call(
            write_out,
            out_shape=shapes,
            in_specs=[vmem] * 5,
            out_specs=(hbm,) * 5,
            scratch_shapes=[dma((5,))],
        )(*[pltpu.with_memory_space_constraint(x, pltpu.VMEM) for x in held])

    in_specs = (
        P("section", "dp", None, None),
        P("dp", "section", None),
        P("dp", "section", None),
        P("section", None),
        P("section", None),
        P("section", "dp", None, None),
        P("dp"),
    )
    out_specs = (
        P("section", "dp", None, None),
        P("dp", "section", None),
        P("dp", "section", None),
        P("section", None),
        P("section", None),
    )
    return jax.shard_map(
        on_device, mesh=mesh, in_specs=in_specs, out_specs=out_specs, check_vma=False
    )
```

```python
import functools
import math

import jax
import jax.numpy as jnp
from jax import lax
from jax.experimental import pallas as pl
from jax.experimental.pallas import tpu as pltpu
from jax.sharding import PartitionSpec as P

HEAD = 128
LAG = 2
DIRECT = 16
NEAR = 4
MESH = pl.DeviceIdType.MESH
BF = jnp.bfloat16
F32 = jnp.float32
NT = (((1,), (1,)), ((), ()))


def radices(n):
    out = []
    while n > 1:
        r = next((r for r in range(DIRECT, 1, -1) if n % r == 0), n)
        out.append(r)
        n //= r
    return out


def near_split(stages):
    if len(stages) == 1 and stages[0] % NEAR == 0:
        return NEAR, stages[0] // NEAR
    return 0, 0


def kernel(
    sections, replicas, stages,
    doc_hbm, q_hbm, k_hbm, v_hbm, qs_hbm, ks_hbm, do_hbm,
    dq_ref, kg_ref, vg_ref, qgain_ref, kgain_ref,
    doc_ref, qs_ref, ks_ref, q_vm, do_vm, k_vm, v_vm, ql_vm, qf_vm, sbuf, dbuf, pbuf, dsbuf, bias, grad, gsend, grecv, *rest,
):
    n_st = len(stages)
    slots = rest[:n_st]
    (small_sem, q_sem, do_sem, kl_sem, vl_sem, kv_ss, kv_rs, g_ss, g_rs) = rest[n_st:n_st + 9]
    st_ss = rest[n_st + 9:2 * n_st + 9]
    st_rs = rest[2 * n_st + 9:3 * n_st + 9]
    reply_sem = rest[3 * n_st + 9]
    line_sems = rest[3 * n_st + 10:]
    groups, length, width = q_vm.shape
    per = width // HEAD
    rows = k_hbm.shape[1]
    half = length // 2
    scale = HEAD ** -0.5
    to_exp2 = scale * math.log2(math.e)
    sec = lax.axis_index("section")
    dp = lax.axis_index("dp")

    def sec_peer(off):
        return lax.rem(sec + off, sections)

    strides = []
    stride = 1
    for r in stages:
        strides.append(stride)
        stride *= r

    def member(s):
        return lax.rem(dp // strides[s], stages[s])

    def st_peer(s, off):
        mine = member(s)
        other = lax.rem(mine + off, stages[s])
        return dp + (other - mine) * strides[s]

    near, far = near_split(stages)
    row, seat = (dp // near, lax.rem(dp, near)) if near else (0, 0)

    def dp_signal(sem, when, offset):
        @pl.when(when)
        def _():
            pl.semaphore_signal(sem, inc=1, device_id={"dp": dp + offset}, device_id_type=MESH)

    def signal_up(sem):
        dp_signal(sem, row < far - 1, near)
        for off in range(1, near):
            dp_signal(sem, seat < near - off, off)

    def signal_down(sem):
        dp_signal(sem, row > 0, -near)
        for off in range(1, near):
            dp_signal(sem, seat >= off, -off)

    def line_signal(sem):
        dp_signal(sem, row > 0, -near)
        dp_signal(sem, row < far - 1, near)

    below = jnp.where(row > 0, 1, 0)
    above = jnp.where(row < far - 1, 1, 0)
    barrier = pltpu.get_barrier_semaphore()
    count = 0
    for off in range(1, sections):
        pl.semaphore_signal(barrier, inc=1, device_id={"section": sec_peer(off)}, device_id_type=MESH)
        count += 1
    if near:
        signal_up(barrier)
        count = count + below + seat
    else:
        for s in range(n_st):
            for off in range(1, stages[s]):
                pl.semaphore_signal(barrier, inc=1, device_id={"dp": st_peer(s, off)}, device_id_type=MESH)
                count += 1

    my_rows = pl.ds(pl.multiple_of(sec * rows, rows), rows)

    def hcols(g):
        return pl.ds(pl.multiple_of(g * HEAD, HEAD), HEAD)

    def wcols(g):
        return pl.ds(pl.multiple_of(g * width, HEAD), width)

    def local_in(g):
        return (
            pltpu.make_async_copy(k_hbm.at[0, :, hcols(g)], k_vm.at[g, my_rows, :], kl_sem.at[g]),
            pltpu.make_async_copy(v_hbm.at[0, :, hcols(g)], v_vm.at[g, my_rows, :], vl_sem.at[g]),
            pltpu.make_async_copy(do_hbm.at[0, 0, :, wcols(g)], do_vm.at[g], do_sem.at[g]),
        )

    def q_in(g):
        return pltpu.make_async_copy(q_hbm.at[0, 0, :, wcols(g)], q_vm.at[g], q_sem.at[g])

    def kv_copies(g, off):
        made = []
        for src, dst in ((k_hbm, k_vm), (v_hbm, v_vm)):
            made.append(pltpu.make_async_remote_copy(
                src_ref=src.at[0, :, hcols(g)],
                dst_ref=dst.at[g, my_rows, :],
                send_sem=kv_ss.at[off - 1],
                recv_sem=kv_rs.at[off - 1, g],
                device_id={"section": sec_peer(off)},
                device_id_type=MESH,
            ))
        return made

    def grad_copy(g, off):
        peer = sec_peer(off)
        return pltpu.make_async_remote_copy(
            src_ref=gsend.at[g, pl.ds(pl.multiple_of(peer * rows, rows), rows), :],
            dst_ref=grecv.at[off - 1, g],
            send_sem=g_ss.at[off - 1],
            recv_sem=g_rs.at[off - 1, g],
            device_id={"section": peer},
            device_id_type=MESH,
        )

    def st_copy(s, g, off):
        mine = member(s)
        return pltpu.make_async_remote_copy(
            src_ref=slots[s].at[g, mine],
            dst_ref=slots[s].at[g, mine],
            send_sem=st_ss[s],
            recv_sem=st_rs[s].at[g],
            device_id={"dp": st_peer(s, off)},
            device_id_type=MESH,
        )

    def drain(ref, sem):
        pltpu.make_async_copy(ref, ref, sem).wait()

    def st_total(s, g):
        drain(slots[s].at[g, :stages[s] - 1], st_rs[s].at[g])
        total = slots[s][g, 0].astype(F32)
        for m in range(1, stages[s]):
            total = total + slots[s][g, m].astype(F32)
        return total

    def st_start(s, g):
        for off in range(1, stages[s]):
            st_copy(s, g, off).start()

    def st_send(s, g, value):
        slots[s][g, member(s)] = value.astype(BF)
        st_start(s, g)

    small = [
        pltpu.make_async_copy(src, dst, small_sem.at[i])
        for i, (src, dst) in enumerate(((doc_hbm, doc_ref), (qs_hbm, qs_ref), (ks_hbm, ks_ref)))
    ]
    for c in small:
        c.start()

    @pl.loop(0, groups)
    def _(g):
        q_in(g).start()
        for c in local_in(g):
            c.start()

    pl.semaphore_wait(barrier, count)

    def send_kv():
        for g in range(groups):
            for off in range(1, sections):
                for c in kv_copies(g, off):
                    c.start()

    second = lax.rem(dp, 2) == 1

    @pl.when(jnp.logical_not(second))
    def _():
        send_kv()

    if near:
        signal_down(reply_sem)

    for c in small:
        c.wait()
    doc = doc_ref[0]
    j_pos = lax.broadcasted_iota(jnp.int32, (length, length), 0)
    i_pos = lax.broadcasted_iota(jnp.int32, (length, length), 1)
    visible = (j_pos <= i_pos) & ((i_pos < doc) | (j_pos >= doc))
    shade = jnp.where(visible, 0.0, -1e30).astype(F32)
    bias[0] = shade[:half, :half]
    bias[1] = shade[:half, half:]
    bias[2] = shade[half:, half:]

    def prepare(g):
        q_in(g).wait()
        for h in range(per):
            q_f = q_vm[g, :, h * HEAD:(h + 1) * HEAD].astype(F32)
            q_scale = qs_ref[:, pl.ds(pl.multiple_of(g * width + h * HEAD, HEAD), HEAD)]
            qf_vm[g, h] = q_f
            ql_vm[g, h] = (q_f * q_scale).astype(BF)

    prepare(0)

    @pl.when(second)
    def _():
        send_kv()

    pl.loop(1, groups)(prepare)
    if near:
        replies = above + near - 1 - seat

        @pl.when(replies > 0)
        def _():
            pl.semaphore_wait(reply_sem, replies)
    for i, sem in enumerate(line_sems[:2]):
        if i:
            pl.semaphore_wait(line_sems[i - 1], below + above)
        line_signal(sem)
    early = len(line_sems[1:])

    def one_group(g, carry):
        for c in local_in(g):
            c.wait()
        for off in range(1, sections):
            drain(grecv.at[off - 1, g], kv_rs.at[off - 1, g])
        k_scale = ks_ref[:, hcols(g)]
        k_raw = k_vm[g].astype(F32)
        k_low = (k_raw * k_scale).astype(BF)
        k_t = k_low.astype(F32).T.astype(BF)
        val = v_vm[g]
        k0, k1 = k_low[:half], k_low[half:]
        v0, v1 = val[:half], val[half:]
        gain_rows = []

        def d_out_of(h):
            return do_vm[g, :, h * HEAD:(h + 1) * HEAD]

        def scores(h):
            q_low = ql_vm[g, h]
            x = lax.dot_general(k0, q_low, NT, preferred_element_type=F32)
            sbuf[h % 2, 0], sbuf[h % 2, 1] = x[:, :half], x[:, half:]
            sbuf[h % 2, 2] = lax.dot_general(k1, q_low[half:], NT, preferred_element_type=F32)

        def d_probs(h):
            d_out = d_out_of(h)
            x = lax.dot_general(v0, d_out, NT, preferred_element_type=F32)
            dbuf[h % 2, 0], dbuf[h % 2, 1] = x[:, :half], x[:, half:]
            dbuf[h % 2, 2] = lax.dot_general(v1, d_out[half:], NT, preferred_element_type=F32)

        def softmax(h, blocks):
            b = h % 2
            xs = [sbuf[b, i] + bias[i] for i in blocks]
            top = functools.reduce(jnp.maximum, xs)
            top = jnp.max(top, axis=0, keepdims=True)
            es = [jnp.exp2((x - top) * to_exp2) for x in xs]
            inv = 1.0 / jnp.sum(functools.reduce(jnp.add, es), axis=0, keepdims=True)
            ps = [e * inv for e in es]
            r = [p * dbuf[b, i] for p, i in zip(ps, blocks)]
            r = jnp.sum(functools.reduce(jnp.add, r), axis=0, keepdims=True)
            for p, i in zip(ps, blocks):
                pbuf[b, i] = p.astype(BF)
                dsbuf[b, i] = (p * (dbuf[b, i] - r)).astype(BF)

        def wide(ref, h):
            return jnp.concatenate([ref[h % 2, 0], ref[h % 2, 1]], axis=1)

        def add(h, rows_, cols_, x):
            if h == 0:
                grad[g, rows_, cols_] = x
            else:
                grad[g, rows_, cols_] += x

        lo, hi = slice(0, half), slice(half, 2 * half)
        kc, vc = slice(0, HEAD), slice(HEAD, 2 * HEAD)

        def kv_grads(h):
            d_out, q_low = d_out_of(h), ql_vm[g, h]
            add(h, lo, vc, jnp.dot(wide(pbuf, h), d_out, preferred_element_type=F32))
            add(h, hi, vc, jnp.dot(pbuf[h % 2, 2], d_out[half:], preferred_element_type=F32))
            add(h, lo, kc, jnp.dot(wide(dsbuf, h), q_low, preferred_element_type=F32))
            add(h, hi, kc, jnp.dot(dsbuf[h % 2, 2], q_low[half:], preferred_element_type=F32))

        def q_grads(h):
            ds_full = jnp.concatenate(
                [wide(dsbuf, h), jnp.concatenate([jnp.zeros((half, half), BF), dsbuf[h % 2, 2]], axis=1)], axis=0
            )
            cols = pl.ds(pl.multiple_of(g * width + h * HEAD, HEAD), HEAD)
            dq = jnp.dot(k_t, ds_full, preferred_element_type=F32).T
            dq_ref[0, 0, :, cols] = (dq * (qs_ref[:, cols] * scale)).astype(BF)
            gain_rows.append(jnp.sum(dq * qf_vm[g, h], axis=0, keepdims=True))

        scores(0)
        d_probs(0)
        for h in range(per):
            if h + 1 < per:
                scores(h + 1)
            softmax(h, (0,))
            if h + 1 < per:
                d_probs(h + 1)
            if h:
                kv_grads(h - 1)
            softmax(h, (1, 2))
            if h:
                q_grads(h - 1)
        kv_grads(per - 1)
        q_grads(per - 1)
        dk = grad[g, :, :HEAD]
        key_term = dk * (k_scale * scale)
        grad[g, :, :HEAD] = key_term
        gsend[g, :, :HEAD] = key_term.astype(BF)
        gsend[g, :, HEAD:] = grad[g, :, HEAD:].astype(BF)
        for off in range(1, sections):
            grad_copy(g, off).start()
        gain_rows.append(jnp.sum(dk * k_raw, axis=0, keepdims=True))
        spare = slots[0].shape[2] - len(gain_rows)
        if spare:
            gain_rows.append(jnp.zeros((spare, HEAD), F32))
        gain_block = jnp.concatenate(gain_rows, axis=0)
        slots[0][g, member(0)] = gain_block.astype(BF)
        for i in range(early):
            @pl.when(g == i)
            def _():
                pl.semaphore_wait(line_sems[i + 1], below + above)
                if i + 1 < early:
                    line_signal(line_sems[i + 2])
        hold = max(early - 1, 0)

        @pl.when(g == hold)
        def _():
            for e in range(hold):
                st_start(0, e)

        @pl.when(g >= hold)
        def _():
            st_start(0, g)

        for s in range(1, n_st):
            @pl.when(g >= LAG * s)
            def _():
                st_send(s, g - LAG * s, st_total(s - 1, g - LAG * s))
        return carry

    lax.fori_loop(0, groups, one_group, 0)

    def finish_gain(g):
        total = st_total(n_st - 1, g) * (scale / replicas)
        for h in range(per):
            qgain_ref[:, (g * per + h) * HEAD:(g * per + h + 1) * HEAD] = total[h:h + 1]
        kgain_ref[:, g * HEAD:(g + 1) * HEAD] = total[per:per + 1]

    def finish_grad(g):
        total = grad[g, my_rows, :]
        for off in range(1, sections):
            grad_copy(g, off).wait_recv()
            total = total + grecv[off - 1, g].astype(F32)
        kg_ref[0, :, g * HEAD:(g + 1) * HEAD] = total[:, :HEAD].astype(BF)
        vg_ref[0, :, g * HEAD:(g + 1) * HEAD] = total[:, HEAD:].astype(BF)

    for t in range(groups, groups + LAG * (n_st - 1)):
        for s in range(n_st - 1, 0, -1):
            g = t - LAG * s
            if 0 <= g < groups:
                st_send(s, g, st_total(s - 1, g))
    for g in range(groups):
        finish_grad(g)
    for g in range(groups):
        finish_gain(g)

    for off in range(1, sections):
        drain(grecv.at[off - 1], kv_ss.at[off - 1])
        drain(grecv.at[off - 1], g_ss.at[off - 1])
    for s in range(n_st):
        drain(slots[s].at[:, :stages[s] - 1], st_ss[s])


def write_out(*refs):
    n = len(refs) // 2
    sems = refs[-1]
    copies = [pltpu.make_async_copy(refs[i], refs[n + i], sems.at[i]) for i in range(n)]
    for c in copies:
        c.start()
    for c in copies:
        c.wait()


def solution(mesh):
    sections = mesh.shape["section"]
    replicas = mesh.shape["dp"]
    stages = radices(replicas)
    n_st = len(stages)

    def on_device(queries, keys, values, query_gain, key_channel_scale, out_grad, doc_start):
        length = queries.shape[2]
        rows, kv_width = keys.shape[1], keys.shape[2]
        groups, half = kv_width // HEAD, length // 2
        width = queries.shape[3] // groups
        gain_rows = -(-(width // HEAD + 1) // 8) * 8
        vmem = pl.BlockSpec(memory_space=pltpu.VMEM)
        hbm = pl.BlockSpec(memory_space=pl.ANY)
        dma = pltpu.SemaphoreType.DMA
        peers = sections - 1
        scratch = [
            pltpu.SMEM(doc_start.shape, jnp.int32),
            pltpu.VMEM(query_gain.shape, F32),
            pltpu.VMEM(key_channel_scale.shape, F32),
            pltpu.VMEM((groups, length, width), BF),
            pltpu.VMEM((groups, length, width), BF),
            pltpu.VMEM((groups, length, HEAD), BF),
            pltpu.VMEM((groups, length, HEAD), BF),
            pltpu.VMEM((groups, width // HEAD, length, HEAD), BF),
            pltpu.VMEM((groups, width // HEAD, length, HEAD), F32),
            pltpu.VMEM((2, 3, half, half), F32),
            pltpu.VMEM((2, 3, half, half), F32),
            pltpu.VMEM((2, 3, half, half), BF),
            pltpu.VMEM((2, 3, half, half), BF),
            pltpu.VMEM((3, half, half), F32),
            pltpu.VMEM((groups, length, 2 * HEAD), F32),
            pltpu.VMEM((groups, length, 2 * HEAD), BF),
            pltpu.VMEM((peers, groups, rows, 2 * HEAD), BF),
        ]
        scratch += [pltpu.VMEM((groups, r, gain_rows, HEAD), BF) for r in stages]
        scratch += [dma((3,))] + [dma((groups,))] * 4
        scratch += [dma((peers,)), dma((peers, groups))] * 2
        scratch += [dma] * n_st + [dma((groups,))] * n_st
        scratch += [pltpu.SemaphoreType.REGULAR] * max(near_split(stages)[1], 1)
        shapes = (
            jax.ShapeDtypeStruct(queries.shape, BF),
            jax.ShapeDtypeStruct(keys.shape, BF),
            jax.ShapeDtypeStruct(values.shape, BF),
            jax.ShapeDtypeStruct(query_gain.shape, F32),
            jax.ShapeDtypeStruct(key_channel_scale.shape, F32),
        )
        held = pl.pallas_call(
            functools.partial(kernel, sections, replicas, stages),
            out_shape=tuple(pltpu.VMEM(x.shape, x.dtype) for x in shapes),
            in_specs=[pl.BlockSpec(memory_space=pltpu.HBM)] + [hbm] * 6,
            out_specs=(vmem,) * 5,
            scratch_shapes=scratch,
            compiler_params=pltpu.CompilerParams(collective_id=0, has_side_effects=True),
        )(doc_start, queries, keys, values, query_gain, key_channel_scale, out_grad)
        return pl.pallas_call(
            write_out,
            out_shape=shapes,
            in_specs=[vmem] * 5,
            out_specs=(hbm,) * 5,
            scratch_shapes=[dma((5,))],
        )(*[pltpu.with_memory_space_constraint(x, pltpu.VMEM) for x in held])

    in_specs = (
        P("section", "dp", None, None),
        P("dp", "section", None),
        P("dp", "section", None),
        P("section", None),
        P("section", None),
        P("section", "dp", None, None),
        P("dp"),
    )
    out_specs = (
        P("section", "dp", None, None),
        P("dp", "section", None),
        P("dp", "section", None),
        P("section", None),
        P("section", None),
    )
    return jax.shard_map(
        on_device, mesh=mesh, in_specs=in_specs, out_specs=out_specs, check_vma=False
    )
```

```python
import functools
import math

import jax
import jax.numpy as jnp
from jax import lax
from jax.experimental import pallas as pl
from jax.experimental.pallas import tpu as pltpu
from jax.sharding import PartitionSpec as P

HEAD = 128
LAG = 2
DIRECT = 16
NEAR = 4
MESH = pl.DeviceIdType.MESH
BF = jnp.bfloat16
F32 = jnp.float32
NT = (((1,), (1,)), ((), ()))


def radices(n):
    out = []
    while n > 1:
        r = next((r for r in range(DIRECT, 1, -1) if n % r == 0), n)
        out.append(r)
        n //= r
    return out


def near_split(stages):
    if len(stages) == 1 and stages[0] % NEAR == 0:
        return NEAR, stages[0] // NEAR
    return 0, 0


def kernel(
    sections, replicas, stages,
    doc_hbm, q_hbm, k_hbm, v_hbm, qs_hbm, ks_hbm, do_hbm,
    dq_ref, kg_ref, vg_ref, qgain_ref, kgain_ref,
    doc_ref, qs_ref, ks_ref, q_vm, do_vm, k_vm, v_vm, ql_vm, qf_vm, sbuf, dbuf, pbuf, dsbuf, bias, grad, gsend, grecv, *rest,
):
    n_st = len(stages)
    slots = rest[:n_st]
    (small_sem, q_sem, do_sem, k_sem, v_sem, out_sem, g_rs) = rest[n_st:n_st + 7]
    st_ss = rest[n_st + 7:2 * n_st + 7]
    st_rs = rest[2 * n_st + 7:3 * n_st + 7]
    reply_sem = rest[3 * n_st + 7]
    line_sems = rest[3 * n_st + 8:]
    groups, length, width = q_vm.shape
    per = width // HEAD
    rows = k_hbm.shape[1]
    half = length // 2
    scale = HEAD ** -0.5
    to_exp2 = scale * math.log2(math.e)
    sec = lax.axis_index("section")
    dp = lax.axis_index("dp")

    def sec_peer(off):
        return lax.rem(sec + off, sections)

    strides = []
    stride = 1
    for r in stages:
        strides.append(stride)
        stride *= r

    def member(s):
        return lax.rem(dp // strides[s], stages[s])

    def st_peer(s, off):
        mine = member(s)
        other = lax.rem(mine + off, stages[s])
        return dp + (other - mine) * strides[s]

    near, far = near_split(stages)
    row, seat = (dp // near, lax.rem(dp, near)) if near else (0, 0)

    def dp_signal(sem, when, offset):
        @pl.when(when)
        def _():
            pl.semaphore_signal(sem, inc=1, device_id={"dp": dp + offset}, device_id_type=MESH)

    def signal_up(sem):
        dp_signal(sem, row < far - 1, near)
        for off in range(1, near):
            dp_signal(sem, seat < near - off, off)

    def signal_down(sem):
        dp_signal(sem, row > 0, -near)
        for off in range(1, near):
            dp_signal(sem, seat >= off, -off)

    def line_signal(sem):
        dp_signal(sem, row > 0, -near)
        dp_signal(sem, row < far - 1, near)

    below = jnp.where(row > 0, 1, 0)
    above = jnp.where(row < far - 1, 1, 0)
    barrier = pltpu.get_barrier_semaphore()
    count = 0
    for off in range(1, sections):
        pl.semaphore_signal(barrier, inc=1, device_id={"section": sec_peer(off)}, device_id_type=MESH)
        count += 1
    if near:
        signal_up(barrier)
        count = count + below + seat
    else:
        for s in range(n_st):
            for off in range(1, stages[s]):
                pl.semaphore_signal(barrier, inc=1, device_id={"dp": st_peer(s, off)}, device_id_type=MESH)
                count += 1

    my_rows = pl.ds(pl.multiple_of(sec * rows, rows), rows)

    def hcols(g):
        return pl.ds(pl.multiple_of(g * HEAD, HEAD), HEAD)

    def wcols(g):
        return pl.ds(pl.multiple_of(g * width, HEAD), width)

    def local_in(g):
        return (
            pltpu.make_async_copy(k_hbm.at[0, :, hcols(g)], k_vm.at[g, my_rows, :], k_sem.at[g]),
            pltpu.make_async_copy(v_hbm.at[0, :, hcols(g)], v_vm.at[g, my_rows, :], v_sem.at[g]),
            pltpu.make_async_copy(q_hbm.at[0, 0, :, wcols(g)], q_vm.at[g], q_sem),
            pltpu.make_async_copy(do_hbm.at[0, 0, :, wcols(g)], do_vm.at[g], do_sem),
        )

    def kv_copies(g, off):
        made = []
        for src, dst, sem in ((k_hbm, k_vm, k_sem), (v_hbm, v_vm, v_sem)):
            made.append(pltpu.make_async_remote_copy(
                src_ref=src.at[0, :, hcols(g)],
                dst_ref=dst.at[g, my_rows, :],
                send_sem=out_sem.at[off - 1],
                recv_sem=sem.at[g],
                device_id={"section": sec_peer(off)},
                device_id_type=MESH,
            ))
        return made

    def grad_copy(g, off):
        peer = sec_peer(off)
        return pltpu.make_async_remote_copy(
            src_ref=gsend.at[g, pl.ds(pl.multiple_of(peer * rows, rows), rows), :],
            dst_ref=grecv.at[off - 1, g],
            send_sem=out_sem.at[off - 1],
            recv_sem=g_rs.at[off - 1],
            device_id={"section": peer},
            device_id_type=MESH,
        )

    def arrival(g):
        return g if n_st > 1 else jnp.where(g == groups - 1, 1, 0)

    def st_copy(s, g, off):
        mine = member(s)
        return pltpu.make_async_remote_copy(
            src_ref=slots[s].at[g, mine],
            dst_ref=slots[s].at[g, mine],
            send_sem=st_ss[s],
            recv_sem=st_rs[s].at[arrival(g)],
            device_id={"dp": st_peer(s, off)},
            device_id_type=MESH,
        )

    def drain(ref, sem):
        pltpu.make_async_copy(ref, ref, sem).wait()

    def slot_sum(s, g):
        total = slots[s][g, 0].astype(F32)
        for m in range(1, stages[s]):
            total = total + slots[s][g, m].astype(F32)
        return total

    def st_total(s, g):
        drain(slots[s].at[g, :stages[s] - 1], st_rs[s].at[g])
        return slot_sum(s, g)

    def st_start(s, g):
        for off in range(1, stages[s]):
            st_copy(s, g, off).start()

    def st_send(s, g, value):
        slots[s][g, member(s)] = value.astype(BF)
        st_start(s, g)

    small = [
        pltpu.make_async_copy(src, dst, small_sem.at[i])
        for i, (src, dst) in enumerate(((doc_hbm, doc_ref), (qs_hbm, qs_ref), (ks_hbm, ks_ref)))
    ]
    for c in small:
        c.start()

    @pl.loop(0, groups)
    def _(g):
        for c in local_in(g):
            c.start()

    pl.semaphore_wait(barrier, count)

    def send_kv(first, last):
        for g in range(first, last):
            for off in range(1, sections):
                for c in kv_copies(g, off):
                    c.start()

    second = lax.rem(dp, 2) == 1
    send_kv(0, 1)

    @pl.when(jnp.logical_not(second))
    def _():
        send_kv(1, groups)

    if near:
        signal_down(reply_sem)

    for c in small:
        c.wait()
    doc = doc_ref[0]
    j_pos = lax.broadcasted_iota(jnp.int32, (length, length), 0)
    i_pos = lax.broadcasted_iota(jnp.int32, (length, length), 1)
    visible = (j_pos <= i_pos) & ((i_pos < doc) | (j_pos >= doc))
    shade = jnp.where(visible, 0.0, -1e30).astype(F32)
    bias[0] = shade[:half, :half]
    bias[1] = shade[:half, half:]
    bias[2] = shade[half:, half:]

    drain(q_vm, q_sem)

    def prepare(g):
        for h in range(per):
            q_f = q_vm[g, :, h * HEAD:(h + 1) * HEAD].astype(F32)
            q_scale = qs_ref[:, pl.ds(pl.multiple_of(g * width + h * HEAD, HEAD), HEAD)]
            qf_vm[g, h] = q_f
            ql_vm[g, h] = (q_f * q_scale).astype(BF)

    pl.loop(0, groups)(prepare)

    @pl.when(second)
    def _():
        send_kv(1, groups)

    if near:
        replies = above + near - 1 - seat

        @pl.when(replies > 0)
        def _():
            pl.semaphore_wait(reply_sem, replies)
    if line_sems:
        line_signal(line_sems[0])

    drain(do_vm, do_sem)
    if line_sems:
        pl.semaphore_wait(line_sems[0], below + above)
    if line_sems[1:]:
        line_signal(line_sems[1])
    early = len(line_sems[1:])

    def when(cond):
        if isinstance(cond, bool):
            return lambda f: f() if cond else None
        return pl.when(cond)

    def one_group(g, last):
        drain(k_vm.at[g], k_sem.at[g])
        drain(v_vm.at[g], v_sem.at[g])
        k_scale = ks_ref[:, hcols(g)]
        k_low = (k_vm[g].astype(F32) * k_scale).astype(BF)
        k_t = k_low.astype(F32).T.astype(BF)
        k0, k1 = k_low[:half], k_low[half:]
        gain_rows = []

        def d_out_of(h):
            return do_vm[g, :, h * HEAD:(h + 1) * HEAD]

        def scores(h):
            q_low = ql_vm[g, h]
            x = lax.dot_general(k0, q_low, NT, preferred_element_type=F32)
            sbuf[h % 2, 0], sbuf[h % 2, 1] = x[:, :half], x[:, half:]
            sbuf[h % 2, 2] = lax.dot_general(k1, q_low[half:], NT, preferred_element_type=F32)

        def d_probs(h):
            d_out = d_out_of(h)
            x = lax.dot_general(v_vm[g, :half], d_out, NT, preferred_element_type=F32)
            dbuf[h % 2, 0], dbuf[h % 2, 1] = x[:, :half], x[:, half:]
            dbuf[h % 2, 2] = lax.dot_general(v_vm[g, half:], d_out[half:], NT, preferred_element_type=F32)

        def softmax(h, blocks):
            b = h % 2
            xs = [sbuf[b, i] + bias[i] for i in blocks]
            top = functools.reduce(jnp.maximum, xs)
            top = jnp.max(top, axis=0, keepdims=True)
            es = [jnp.exp2((x - top) * to_exp2) for x in xs]
            inv = 1.0 / jnp.sum(functools.reduce(jnp.add, es), axis=0, keepdims=True)
            ps = [e * inv for e in es]
            r = [p * dbuf[b, i] for p, i in zip(ps, blocks)]
            r = jnp.sum(functools.reduce(jnp.add, r), axis=0, keepdims=True)
            for p, i in zip(ps, blocks):
                pbuf[h, i] = p.astype(BF)
                dsbuf[h, i] = (p * (dbuf[b, i] - r)).astype(BF)

        def wide(ref, h):
            return jnp.concatenate([ref[h, 0], ref[h, 1]], axis=1)

        def add(h, rows_, cols_, x):
            if h == 0:
                grad[g, rows_, cols_] = x
            else:
                grad[g, rows_, cols_] += x

        lo, hi = slice(0, half), slice(half, 2 * half)
        kc, vc = slice(0, HEAD), slice(HEAD, 2 * HEAD)

        def kv_grads(h):
            d_out, q_low = d_out_of(h), ql_vm[g, h]
            add(h, lo, vc, jnp.dot(wide(pbuf, h), d_out, preferred_element_type=F32))
            add(h, hi, vc, jnp.dot(pbuf[h, 2], d_out[half:], preferred_element_type=F32))
            add(h, lo, kc, jnp.dot(wide(dsbuf, h), q_low, preferred_element_type=F32))
            add(h, hi, kc, jnp.dot(dsbuf[h, 2], q_low[half:], preferred_element_type=F32))

        def q_grads(h):
            ds_full = jnp.concatenate(
                [wide(dsbuf, h), jnp.concatenate([jnp.zeros((half, half), BF), dsbuf[h, 2]], axis=1)], axis=0
            )
            cols = pl.ds(pl.multiple_of(g * width + h * HEAD, HEAD), HEAD)
            dq = jnp.dot(k_t, ds_full, preferred_element_type=F32).T
            dq_ref[0, 0, :, cols] = (dq * (qs_ref[:, cols] * scale)).astype(BF)
            gain_rows.append(jnp.sum(dq * qf_vm[g, h], axis=0, keepdims=True))

        def all_kv_grads():
            heads = range(per)
            for ref, right, cols in (
                (pbuf, [d_out_of(h) for h in heads], vc),
                (dsbuf, [ql_vm[g, h] for h in heads], kc),
            ):
                grad[g, lo, cols] = jnp.dot(
                    jnp.concatenate([wide(ref, h) for h in heads], axis=1),
                    jnp.concatenate(right, axis=0), preferred_element_type=F32,
                )
                grad[g, hi, cols] = jnp.dot(
                    jnp.concatenate([ref[h, 2] for h in heads], axis=1),
                    jnp.concatenate([x[half:] for x in right], axis=0), preferred_element_type=F32,
                )

        def send_grads():
            key_term = grad[g, :, kc] * (k_scale * scale)
            grad[g, :, kc] = key_term
            gsend[g, :, kc] = key_term.astype(BF)
            gsend[g, :, vc] = grad[g, :, vc].astype(BF)
            for off in range(1, sections):
                grad_copy(g, off).start()

        def send_gains():
            spare = slots[0].shape[2] - per
            rows_ = gain_rows + ([jnp.zeros((spare, HEAD), F32)] if spare else [])
            slots[0][g, member(0)] = jnp.concatenate(rows_, axis=0).astype(BF)
            for i in range(early):
                @when(g == i)
                def _():
                    pl.semaphore_wait(line_sems[i + 1], below + above)
                    if i + 1 < early:
                        line_signal(line_sems[i + 2])
            hold = max(early - 1, 0)

            @when(g == hold)
            def _():
                for e in range(hold):
                    st_start(0, e)

            @when(g >= hold)
            def _():
                st_start(0, g)

        scores(0)
        d_probs(0)
        for h in range(per):
            if h + 1 < per:
                scores(h + 1)
            softmax(h, (0,))
            if h + 1 < per:
                d_probs(h + 1)
            if h and not last:
                kv_grads(h - 1)
            softmax(h, (1, 2))
            if h:
                q_grads(h - 1)
        if last:
            q_grads(per - 1)
            send_gains()
            all_kv_grads()
            send_grads()
        else:
            kv_grads(per - 1)
            q_grads(per - 1)
            send_grads()
            send_gains()

        for s in range(1, n_st):
            @when(g >= LAG * s)
            def _():
                st_send(s, g - LAG * s, st_total(s - 1, g - LAG * s))

    pl.loop(0, groups - 1)(lambda g: one_group(g, False))
    one_group(groups - 1, True)

    def finish_gain(g, total):
        total = total * (scale / replicas)
        key_sum = 0.0
        for h in range(per):
            cols = slice((g * per + h) * HEAD, (g * per + h + 1) * HEAD)
            qgain_ref[:, cols] = total[h:h + 1]
            key_sum = key_sum + total[h:h + 1] * qs_ref[:, cols]
        cols = slice(g * HEAD, (g + 1) * HEAD)
        kgain_ref[:, cols] = key_sum / ks_ref[:, cols]

    def finish_grad(g):
        total = grad[g, my_rows, :]
        for off in range(1, sections):
            total = total + grecv[off - 1, g].astype(F32)
        kg_ref[0, :, g * HEAD:(g + 1) * HEAD] = total[:, :HEAD].astype(BF)
        vg_ref[0, :, g * HEAD:(g + 1) * HEAD] = total[:, HEAD:].astype(BF)

    for t in range(groups, groups + LAG * (n_st - 1)):
        for s in range(n_st - 1, 0, -1):
            g = t - LAG * s
            if 0 <= g < groups:
                st_send(s, g, st_total(s - 1, g))
    if n_st == 1 and groups > 1:
        drain(slots[0].at[:groups - 1, :stages[0] - 1], st_rs[0].at[0])
        for g in range(groups - 1):
            finish_gain(g, slot_sum(0, g))
    for off in range(1, sections):
        drain(grecv.at[off - 1], g_rs.at[off - 1])
    for g in range(groups):
        finish_grad(g)
    for off in range(1, sections):
        drain(gsend.at[:, :2 * rows], out_sem.at[off - 1])
    if n_st == 1:
        drain(slots[0].at[0, :stages[0] - 1], st_rs[0].at[1])
        finish_gain(groups - 1, slot_sum(0, groups - 1))
    else:
        for g in range(groups):
            finish_gain(g, st_total(n_st - 1, g))

    for s in range(n_st):
        drain(slots[s].at[:, :stages[s] - 1], st_ss[s])


def write_out(*refs):
    n = len(refs) // 2
    sems = refs[-1]
    copies = [pltpu.make_async_copy(refs[i], refs[n + i], sems.at[i]) for i in range(n)]
    for c in copies:
        c.start()
    for c in copies:
        c.wait()


def solution(mesh):
    sections = mesh.shape["section"]
    replicas = mesh.shape["dp"]
    stages = radices(replicas)
    n_st = len(stages)

    def on_device(queries, keys, values, query_gain, key_channel_scale, out_grad, doc_start):
        length = queries.shape[2]
        rows, kv_width = keys.shape[1], keys.shape[2]
        groups, half = kv_width // HEAD, length // 2
        width = queries.shape[3] // groups
        per = width // HEAD
        gain_rows = -(-per // 8) * 8
        vmem = pl.BlockSpec(memory_space=pltpu.VMEM)
        hbm = pl.BlockSpec(memory_space=pl.ANY)
        dma = pltpu.SemaphoreType.DMA
        peers = sections - 1
        scratch = [
            pltpu.SMEM(doc_start.shape, jnp.int32),
            pltpu.VMEM(query_gain.shape, F32),
            pltpu.VMEM(key_channel_scale.shape, F32),
            pltpu.VMEM((groups, length, width), BF),
            pltpu.VMEM((groups, length, width), BF),
            pltpu.VMEM((groups, length, HEAD), BF),
            pltpu.VMEM((groups, length, HEAD), BF),
            pltpu.VMEM((groups, width // HEAD, length, HEAD), BF),
            pltpu.VMEM((groups, width // HEAD, length, HEAD), F32),
            pltpu.VMEM((2, 3, half, half), F32),
            pltpu.VMEM((2, 3, half, half), F32),
            pltpu.VMEM((per, 3, half, half), BF),
            pltpu.VMEM((per, 3, half, half), BF),
            pltpu.VMEM((3, half, half), F32),
            pltpu.VMEM((groups, length, 2 * HEAD), F32),
            pltpu.VMEM((groups, length, 2 * HEAD), BF),
            pltpu.VMEM((peers, groups, rows, 2 * HEAD), BF),
        ]
        scratch += [pltpu.VMEM((groups, r, gain_rows, HEAD), BF) for r in stages]
        scratch += [dma((3,)), dma, dma, dma((groups,)), dma((groups,)), dma((peers,)), dma((peers,))]
        scratch += [dma] * n_st + [dma((groups if n_st > 1 else 2,))] * n_st
        scratch += [pltpu.SemaphoreType.REGULAR] * max(near_split(stages)[1], 1)
        shapes = (
            jax.ShapeDtypeStruct(queries.shape, BF),
            jax.ShapeDtypeStruct(keys.shape, BF),
            jax.ShapeDtypeStruct(values.shape, BF),
            jax.ShapeDtypeStruct(query_gain.shape, F32),
            jax.ShapeDtypeStruct(key_channel_scale.shape, F32),
        )
        held = pl.pallas_call(
            functools.partial(kernel, sections, replicas, stages),
            out_shape=tuple(pltpu.VMEM(x.shape, x.dtype) for x in shapes),
            in_specs=[pl.BlockSpec(memory_space=pltpu.HBM)] + [hbm] * 6,
            out_specs=(vmem,) * 5,
            scratch_shapes=scratch,
            compiler_params=pltpu.CompilerParams(collective_id=0, has_side_effects=True),
        )(doc_start, queries, keys, values, query_gain, key_channel_scale, out_grad)
        return pl.pallas_call(
            write_out,
            out_shape=shapes,
            in_specs=[vmem] * 5,
            out_specs=(hbm,) * 5,
            scratch_shapes=[dma((5,))],
        )(*[pltpu.with_memory_space_constraint(x, pltpu.VMEM) for x in held])

    in_specs = (
        P("section", "dp", None, None),
        P("dp", "section", None),
        P("dp", "section", None),
        P("section", None),
        P("section", None),
        P("section", "dp", None, None),
        P("dp"),
    )
    out_specs = (
        P("section", "dp", None, None),
        P("dp", "section", None),
        P("dp", "section", None),
        P("section", None),
        P("section", None),
    )
    return jax.shard_map(
        on_device, mesh=mesh, in_specs=in_specs, out_specs=out_specs, check_vma=False
    )
```

```python
import functools
import math

import jax
import jax.numpy as jnp
from jax import lax
from jax.experimental import pallas as pl
from jax.experimental.pallas import tpu as pltpu
from jax.sharding import PartitionSpec as P

HEAD = 128
LAG = 2
DIRECT = 16
NEAR = 4
MESH = pl.DeviceIdType.MESH
BF = jnp.bfloat16
F32 = jnp.float32
NT = (((1,), (1,)), ((), ()))


def radices(n):
    out = []
    while n > 1:
        r = next((r for r in range(DIRECT, 1, -1) if n % r == 0), n)
        out.append(r)
        n //= r
    return out


def near_split(stages):
    if len(stages) == 1 and stages[0] % NEAR == 0:
        return NEAR, stages[0] // NEAR
    return 0, 0


def kernel(
    sections, replicas, stages,
    doc_hbm, q_hbm, k_hbm, v_hbm, qs_hbm, ks_hbm, do_hbm,
    dq_ref, kg_ref, vg_ref, qgain_ref, kgain_ref,
    doc_ref, qs_ref, ks_ref, q_vm, do_vm, k_vm, v_vm, ql_vm, qf_vm, sbuf, dbuf, pbuf, dsbuf, plo, dslo, bias, grad, gsend, grecv, *rest,
):
    n_st = len(stages)
    slots = rest[:n_st]
    (small_sem, q_sem, do_sem, own_sem, kv_sem, out_sem, g_rs) = rest[n_st:n_st + 7]
    st_ss = rest[n_st + 7:2 * n_st + 7]
    st_rs = rest[2 * n_st + 7:3 * n_st + 7]
    reply_sem = rest[3 * n_st + 7]
    line_sems = rest[3 * n_st + 8:]
    groups, length, width = q_vm.shape
    per = width // HEAD
    rows = k_hbm.shape[1]
    half = length // 2
    scale = HEAD ** -0.5
    to_exp2 = scale * math.log2(math.e)
    sec = lax.axis_index("section")
    dp = lax.axis_index("dp")

    def sec_peer(off):
        return lax.rem(sec + off, sections)

    strides = []
    stride = 1
    for r in stages:
        strides.append(stride)
        stride *= r

    def member(s):
        return lax.rem(dp // strides[s], stages[s])

    def st_peer(s, off):
        mine = member(s)
        other = lax.rem(mine + off, stages[s])
        return dp + (other - mine) * strides[s]

    near, far = near_split(stages)
    row, seat = (dp // near, lax.rem(dp, near)) if near else (0, 0)

    def dp_signal(sem, when, offset):
        @pl.when(when)
        def _():
            pl.semaphore_signal(sem, inc=1, device_id={"dp": dp + offset}, device_id_type=MESH)

    def signal_up(sem):
        dp_signal(sem, row < far - 1, near)
        for off in range(1, near):
            dp_signal(sem, seat < near - off, off)

    def signal_down(sem):
        dp_signal(sem, row > 0, -near)
        for off in range(1, near):
            dp_signal(sem, seat >= off, -off)

    def line_signal(sem):
        dp_signal(sem, row > 0, -near)
        dp_signal(sem, row < far - 1, near)

    below = jnp.where(row > 0, 1, 0)
    above = jnp.where(row < far - 1, 1, 0)
    barrier = pltpu.get_barrier_semaphore()
    count = 0
    for off in range(1, sections):
        pl.semaphore_signal(barrier, inc=1, device_id={"section": sec_peer(off)}, device_id_type=MESH)
        count += 1
    if near:
        signal_up(barrier)
        count = count + below + seat
    else:
        for s in range(n_st):
            for off in range(1, stages[s]):
                pl.semaphore_signal(barrier, inc=1, device_id={"dp": st_peer(s, off)}, device_id_type=MESH)
                count += 1

    my_rows = pl.ds(pl.multiple_of(sec * rows, rows), rows)

    def hcols(g):
        return pl.ds(pl.multiple_of(g * HEAD, HEAD), HEAD)

    def wcols(g):
        return pl.ds(pl.multiple_of(g * width, HEAD), width)

    def local_in(g):
        return (
            pltpu.make_async_copy(k_hbm.at[0, :, hcols(g)], k_vm.at[g, my_rows, :], own_sem),
            pltpu.make_async_copy(v_hbm.at[0, :, hcols(g)], v_vm.at[g, my_rows, :], own_sem),
            pltpu.make_async_copy(q_hbm.at[0, 0, :, wcols(g)], q_vm.at[g], q_sem),
            pltpu.make_async_copy(do_hbm.at[0, 0, :, wcols(g)], do_vm.at[g], do_sem),
        )

    def kv_copies(g, off):
        made = []
        for src, dst in ((k_hbm, k_vm), (v_hbm, v_vm)):
            made.append(pltpu.make_async_remote_copy(
                src_ref=src.at[0, :, hcols(g)],
                dst_ref=dst.at[g, my_rows, :],
                send_sem=out_sem.at[off - 1],
                recv_sem=kv_sem.at[g],
                device_id={"section": sec_peer(off)},
                device_id_type=MESH,
            ))
        return made

    def grad_copy(g, off):
        peer = sec_peer(off)
        return pltpu.make_async_remote_copy(
            src_ref=gsend.at[g, pl.ds(pl.multiple_of(peer * rows, rows), rows), :],
            dst_ref=grecv.at[off - 1, g],
            send_sem=out_sem.at[off - 1],
            recv_sem=g_rs.at[off - 1],
            device_id={"section": peer},
            device_id_type=MESH,
        )

    def arrival(g):
        return g if n_st > 1 else jnp.where(g == groups - 1, 1, 0)

    def st_copy(s, g, off):
        mine = member(s)
        return pltpu.make_async_remote_copy(
            src_ref=slots[s].at[g, mine],
            dst_ref=slots[s].at[g, mine],
            send_sem=st_ss[s],
            recv_sem=st_rs[s].at[arrival(g)],
            device_id={"dp": st_peer(s, off)},
            device_id_type=MESH,
        )

    def drain(ref, sem):
        pltpu.make_async_copy(ref, ref, sem).wait()

    def slot_sum(s, g):
        total = slots[s][g, 0].astype(F32)
        for m in range(1, stages[s]):
            total = total + slots[s][g, m].astype(F32)
        return total

    def st_total(s, g):
        drain(slots[s].at[g, :stages[s] - 1], st_rs[s].at[g])
        return slot_sum(s, g)

    def st_start(s, g):
        for off in range(1, stages[s]):
            st_copy(s, g, off).start()

    def st_send(s, g, value):
        slots[s][g, member(s)] = value.astype(BF)
        st_start(s, g)

    small = [
        pltpu.make_async_copy(src, dst, small_sem.at[i])
        for i, (src, dst) in enumerate(((doc_hbm, doc_ref), (qs_hbm, qs_ref), (ks_hbm, ks_ref)))
    ]
    for c in small:
        c.start()

    @pl.loop(0, groups)
    def _(g):
        for c in local_in(g):
            c.start()

    pl.semaphore_wait(barrier, count)

    def send_kv(first, last):
        for g in range(first, last):
            for off in range(1, sections):
                for c in kv_copies(g, off):
                    c.start()

    second = lax.rem(dp, 2) == 1
    send_kv(0, 1)

    @pl.when(jnp.logical_not(second))
    def _():
        send_kv(1, groups)

    if near:
        signal_down(reply_sem)

    for c in small:
        c.wait()
    doc = doc_ref[0]
    j_pos = lax.broadcasted_iota(jnp.int32, (length, length), 0)
    i_pos = lax.broadcasted_iota(jnp.int32, (length, length), 1)
    visible = (j_pos <= i_pos) & ((i_pos < doc) | (j_pos >= doc))
    shade = jnp.where(visible, 0.0, -1e30).astype(F32)
    bias[0] = shade[:half, :half]
    bias[1] = shade[:half, half:]
    bias[2] = shade[half:, half:]

    drain(q_vm, q_sem)

    def prepare(g):
        for h in range(per):
            q_f = q_vm[g, :, h * HEAD:(h + 1) * HEAD].astype(F32)
            q_scale = qs_ref[:, pl.ds(pl.multiple_of(g * width + h * HEAD, HEAD), HEAD)]
            qf_vm[g, h] = q_f
            ql_vm[g, h] = (q_f * q_scale).astype(BF)

    pl.loop(0, groups)(prepare)

    @pl.when(second)
    def _():
        send_kv(1, groups)

    if near:
        replies = above + near - 1 - seat

        @pl.when(replies > 0)
        def _():
            pl.semaphore_wait(reply_sem, replies)
    if line_sems:
        line_signal(line_sems[0])

    drain(do_vm, do_sem)
    drain(grecv.at[0], own_sem)

    def weigh(xs, ds):
        top = jnp.max(functools.reduce(jnp.maximum, xs), axis=0, keepdims=True)
        es = [jnp.exp2((x - top) * to_exp2) for x in xs]
        inv = 1.0 / jnp.sum(functools.reduce(jnp.add, es), axis=0, keepdims=True)
        ps = [e * inv for e in es]
        r = [p * d[...] for p, d in zip(ps, ds)]
        r = jnp.sum(functools.reduce(jnp.add, r), axis=0, keepdims=True)
        return [(p.astype(BF), (p * (d[...] - r)).astype(BF)) for p, d in zip(ps, ds)]

    lead = rows >= half

    def ahead(g):
        k_low = (k_vm[g, :half].astype(F32) * ks_ref[:, hcols(g)]).astype(BF)

        def dots(h):
            d_out = do_vm[g, :half, h * HEAD:(h + 1) * HEAD]
            sbuf[h % 2, 0] = lax.dot_general(k_low, ql_vm[g, h, :half], NT, preferred_element_type=F32)
            dbuf[h % 2, 0] = lax.dot_general(v_vm[g, :half], d_out, NT, preferred_element_type=F32)

        dots(0)
        for h in range(per):
            if h + 1 < per:
                dots(h + 1)
            plo[g, h], dslo[g, h] = weigh([sbuf[h % 2, 0] + bias[0]], [dbuf.at[h % 2, 0]])[0]

    if lead:
        @pl.when(sec == 0)
        def _():
            pl.loop(0, groups)(ahead)

    if line_sems:
        pl.semaphore_wait(line_sems[0], below + above)
    if line_sems[1:]:
        line_signal(line_sems[1])
    early = len(line_sems[1:])

    def when(cond):
        if isinstance(cond, bool):
            return lambda f: f() if cond else None
        return pl.when(cond)

    def one_group(g, last, early_lo):
        drain(grecv.at[:, g], kv_sem.at[g])
        k_scale = ks_ref[:, hcols(g)]
        k_low = (k_vm[g].astype(F32) * k_scale).astype(BF)
        k0, k1 = k_low[:half], k_low[half:]
        gain_rows = []

        def d_out_of(h):
            return do_vm[g, :, h * HEAD:(h + 1) * HEAD]

        def scores(h):
            q_low = ql_vm[g, h]
            if early_lo:
                sbuf[h % 2, 1] = lax.dot_general(k0, q_low[half:], NT, preferred_element_type=F32)
            else:
                x = lax.dot_general(k0, q_low, NT, preferred_element_type=F32)
                sbuf[h % 2, 0], sbuf[h % 2, 1] = x[:, :half], x[:, half:]
            sbuf[h % 2, 2] = lax.dot_general(k1, q_low[half:], NT, preferred_element_type=F32)

        def d_probs(h):
            d_out = d_out_of(h)
            if early_lo:
                dbuf[h % 2, 1] = lax.dot_general(v_vm[g, :half], d_out[half:], NT, preferred_element_type=F32)
            else:
                x = lax.dot_general(v_vm[g, :half], d_out, NT, preferred_element_type=F32)
                dbuf[h % 2, 0], dbuf[h % 2, 1] = x[:, :half], x[:, half:]
            dbuf[h % 2, 2] = lax.dot_general(v_vm[g, half:], d_out[half:], NT, preferred_element_type=F32)

        def softmax(h, blocks):
            b = h % 2
            made = weigh([sbuf[b, i] + bias[i] for i in blocks], [dbuf.at[b, i] for i in blocks])
            for i, (p, ds) in zip(blocks, made):
                if i:
                    pbuf[h, i - 1], dsbuf[h, i - 1] = p, ds
                else:
                    plo[g, h], dslo[g, h] = p, ds

        def wide(ref, h):
            first = plo if ref is pbuf else dslo
            return jnp.concatenate([first[g, h], ref[h, 0]], axis=1)

        def add(h, rows_, cols_, x):
            if h == 0:
                grad[g, rows_, cols_] = x
            else:
                grad[g, rows_, cols_] += x

        lo, hi = slice(0, half), slice(half, 2 * half)
        kc, vc = slice(0, HEAD), slice(HEAD, 2 * HEAD)

        def kv_grads(h):
            d_out, q_low = d_out_of(h), ql_vm[g, h]
            add(h, lo, vc, jnp.dot(wide(pbuf, h), d_out, preferred_element_type=F32))
            add(h, hi, vc, jnp.dot(pbuf[h, 1], d_out[half:], preferred_element_type=F32))
            add(h, lo, kc, jnp.dot(wide(dsbuf, h), q_low, preferred_element_type=F32))
            add(h, hi, kc, jnp.dot(dsbuf[h, 1], q_low[half:], preferred_element_type=F32))

        def q_grads(h):
            cols = pl.ds(pl.multiple_of(g * width + h * HEAD, HEAD), HEAD)
            hi_ds = jnp.concatenate([dsbuf[h, 0], dsbuf[h, 1]], axis=0)
            dq = jnp.concatenate([
                lax.dot_general(dslo[g, h], k_low[:half], (((0,), (0,)), ((), ())), preferred_element_type=F32),
                lax.dot_general(hi_ds, k_low, (((0,), (0,)), ((), ())), preferred_element_type=F32),
            ], axis=0)
            dq_ref[0, 0, :, cols] = (dq * (qs_ref[:, cols] * scale)).astype(BF)
            gain_rows.append(jnp.sum(dq * qf_vm[g, h], axis=0, keepdims=True))

        def all_kv_grads():
            heads = range(per)
            for ref, right, cols in (
                (pbuf, [d_out_of(h) for h in heads], vc),
                (dsbuf, [ql_vm[g, h] for h in heads], kc),
            ):
                grad[g, lo, cols] = jnp.dot(
                    jnp.concatenate([wide(ref, h) for h in heads], axis=1),
                    jnp.concatenate(right, axis=0), preferred_element_type=F32,
                )
                grad[g, hi, cols] = jnp.dot(
                    jnp.concatenate([ref[h, 1] for h in heads], axis=1),
                    jnp.concatenate([x[half:] for x in right], axis=0), preferred_element_type=F32,
                )

        def send_grads():
            key_term = grad[g, :, kc] * (k_scale * scale)
            grad[g, :, kc] = key_term
            gsend[g, :, kc] = key_term.astype(BF)
            gsend[g, :, vc] = grad[g, :, vc].astype(BF)
            for off in range(1, sections):
                grad_copy(g, off).start()

        def send_gains():
            spare = slots[0].shape[2] - per
            rows_ = gain_rows + ([jnp.zeros((spare, HEAD), F32)] if spare else [])
            slots[0][g, member(0)] = jnp.concatenate(rows_, axis=0).astype(BF)
            for i in range(early):
                @when(g == i)
                def _():
                    pl.semaphore_wait(line_sems[i + 1], below + above)
                    if i + 1 < early:
                        line_signal(line_sems[i + 2])
            hold = max(early - 1, 0)

            @when(g == hold)
            def _():
                for e in range(hold):
                    st_start(0, e)

            @when(g >= hold)
            def _():
                st_start(0, g)

        scores(0)
        d_probs(0)
        for h in range(per):
            if h + 1 < per:
                scores(h + 1)
            if not early_lo:
                softmax(h, (0,))
            if h + 1 < per:
                d_probs(h + 1)
            if h and not last:
                kv_grads(h - 1)
            softmax(h, (1, 2))
            if h > 1 and not last:
                q_grads(h - 2)
            if h and last:
                q_grads(h - 1)
        if last:
            q_grads(per - 1)
            send_gains()
            all_kv_grads()
            send_grads()
        else:
            if per > 1:
                q_grads(per - 2)
            kv_grads(per - 1)
            q_grads(per - 1)
            send_grads()
            send_gains()

        for s in range(1, n_st):
            @when(g >= LAG * s)
            def _():
                st_send(s, g - LAG * s, st_total(s - 1, g - LAG * s))

    def all_groups(early_lo):
        pl.loop(0, groups - 1)(lambda g: one_group(g, False, early_lo))
        one_group(groups - 1, True, early_lo)

    if lead:
        @pl.when(sec == 0)
        def _():
            all_groups(True)

        @pl.when(sec != 0)
        def _():
            all_groups(False)
    else:
        all_groups(False)

    def finish_gain(g, total):
        total = total * (scale / replicas)
        key_sum = 0.0
        for h in range(per):
            cols = slice((g * per + h) * HEAD, (g * per + h + 1) * HEAD)
            qgain_ref[:, cols] = total[h:h + 1]
            key_sum = key_sum + total[h:h + 1] * qs_ref[:, cols]
        cols = slice(g * HEAD, (g + 1) * HEAD)
        kgain_ref[:, cols] = key_sum / ks_ref[:, cols]

    def finish_grad(g):
        total = grad[g, my_rows, :]
        for off in range(1, sections):
            total = total + grecv[off - 1, g].astype(F32)
        kg_ref[0, :, g * HEAD:(g + 1) * HEAD] = total[:, :HEAD].astype(BF)
        vg_ref[0, :, g * HEAD:(g + 1) * HEAD] = total[:, HEAD:].astype(BF)

    for t in range(groups, groups + LAG * (n_st - 1)):
        for s in range(n_st - 1, 0, -1):
            g = t - LAG * s
            if 0 <= g < groups:
                st_send(s, g, st_total(s - 1, g))
    if n_st == 1 and groups > 1:
        drain(slots[0].at[:groups - 1, :stages[0] - 1], st_rs[0].at[0])
        for g in range(groups - 1):
            finish_gain(g, slot_sum(0, g))
    for off in range(1, sections):
        drain(grecv.at[off - 1], g_rs.at[off - 1])
    for g in range(groups):
        finish_grad(g)
    for off in range(1, sections):
        drain(gsend.at[:, :2 * rows], out_sem.at[off - 1])
    if n_st == 1:
        drain(slots[0].at[0, :stages[0] - 1], st_rs[0].at[1])
        finish_gain(groups - 1, slot_sum(0, groups - 1))
    else:
        for g in range(groups):
            finish_gain(g, st_total(n_st - 1, g))

    for s in range(n_st):
        drain(slots[s].at[:, :stages[s] - 1], st_ss[s])


def write_out(*refs):
    n = len(refs) // 2
    sems = refs[-1]
    copies = [pltpu.make_async_copy(refs[i], refs[n + i], sems.at[i]) for i in range(n)]
    for c in copies:
        c.start()
    for c in copies:
        c.wait()


def solution(mesh):
    sections = mesh.shape["section"]
    replicas = mesh.shape["dp"]
    stages = radices(replicas)
    n_st = len(stages)

    def on_device(queries, keys, values, query_gain, key_channel_scale, out_grad, doc_start):
        length = queries.shape[2]
        rows, kv_width = keys.shape[1], keys.shape[2]
        groups, half = kv_width // HEAD, length // 2
        width = queries.shape[3] // groups
        per = width // HEAD
        gain_rows = -(-per // 8) * 8
        vmem = pl.BlockSpec(memory_space=pltpu.VMEM)
        hbm = pl.BlockSpec(memory_space=pl.ANY)
        dma = pltpu.SemaphoreType.DMA
        peers = sections - 1
        scratch = [
            pltpu.SMEM(doc_start.shape, jnp.int32),
            pltpu.VMEM(query_gain.shape, F32),
            pltpu.VMEM(key_channel_scale.shape, F32),
            pltpu.VMEM((groups, length, width), BF),
            pltpu.VMEM((groups, length, width), BF),
            pltpu.VMEM((groups, length, HEAD), BF),
            pltpu.VMEM((groups, length, HEAD), BF),
            pltpu.VMEM((groups, width // HEAD, length, HEAD), BF),
            pltpu.VMEM((groups, width // HEAD, length, HEAD), F32),
            pltpu.VMEM((2, 3, half, half), F32),
            pltpu.VMEM((2, 3, half, half), F32),
            pltpu.VMEM((per, 2, half, half), BF),
            pltpu.VMEM((per, 2, half, half), BF),
            pltpu.VMEM((groups, per, half, half), BF),
            pltpu.VMEM((groups, per, half, half), BF),
            pltpu.VMEM((3, half, half), F32),
            pltpu.VMEM((groups, length, 2 * HEAD), F32),
            pltpu.VMEM((groups, length, 2 * HEAD), BF),
            pltpu.VMEM((peers, groups, rows, 2 * HEAD), BF),
        ]
        scratch += [pltpu.VMEM((groups, r, gain_rows, HEAD), BF) for r in stages]
        scratch += [dma((3,)), dma, dma, dma, dma((groups,)), dma((peers,)), dma((peers,))]
        scratch += [dma] * n_st + [dma((groups if n_st > 1 else 2,))] * n_st
        scratch += [pltpu.SemaphoreType.REGULAR] * max(near_split(stages)[1], 1)
        shapes = (
            jax.ShapeDtypeStruct(queries.shape, BF),
            jax.ShapeDtypeStruct(keys.shape, BF),
            jax.ShapeDtypeStruct(values.shape, BF),
            jax.ShapeDtypeStruct(query_gain.shape, F32),
            jax.ShapeDtypeStruct(key_channel_scale.shape, F32),
        )
        held = pl.pallas_call(
            functools.partial(kernel, sections, replicas, stages),
            out_shape=tuple(pltpu.VMEM(x.shape, x.dtype) for x in shapes),
            in_specs=[pl.BlockSpec(memory_space=pltpu.HBM)] + [hbm] * 6,
            out_specs=(vmem,) * 5,
            scratch_shapes=scratch,
            compiler_params=pltpu.CompilerParams(collective_id=0, has_side_effects=True),
        )(doc_start, queries, keys, values, query_gain, key_channel_scale, out_grad)
        return pl.pallas_call(
            write_out,
            out_shape=shapes,
            in_specs=[vmem] * 5,
            out_specs=(hbm,) * 5,
            scratch_shapes=[dma((5,))],
        )(*[pltpu.with_memory_space_constraint(x, pltpu.VMEM) for x in held])

    in_specs = (
        P("section", "dp", None, None),
        P("dp", "section", None),
        P("dp", "section", None),
        P("section", None),
        P("section", None),
        P("section", "dp", None, None),
        P("dp"),
    )
    out_specs = (
        P("section", "dp", None, None),
        P("dp", "section", None),
        P("dp", "section", None),
        P("section", None),
        P("section", None),
    )
    return jax.shard_map(
        on_device, mesh=mesh, in_specs=in_specs, out_specs=out_specs, check_vma=False
    )
```

```python
import functools
import math

import jax
import jax.numpy as jnp
from jax import lax
from jax.experimental import pallas as pl
from jax.experimental.pallas import tpu as pltpu
from jax.sharding import PartitionSpec as P

HEAD = 128
LAG = 2
DIRECT = 16
NEAR = 4
MESH = pl.DeviceIdType.MESH
BF = jnp.bfloat16
F32 = jnp.float32
NT = (((1,), (1,)), ((), ()))


def radices(n):
    out = []
    while n > 1:
        r = next((r for r in range(DIRECT, 1, -1) if n % r == 0), n)
        out.append(r)
        n //= r
    return out


def near_split(stages):
    if len(stages) == 1 and stages[0] % NEAR == 0:
        return NEAR, stages[0] // NEAR
    return 0, 0


def kernel(
    sections, replicas, stages,
    doc_hbm, q_hbm, k_hbm, v_hbm, qs_hbm, ks_hbm, do_hbm,
    dq_ref, kg_ref, vg_ref, qgain_ref, kgain_ref,
    doc_ref, qs_ref, ks_ref, q_vm, do_vm, k_vm, v_vm, ql_vm, qf_vm, sbuf, dbuf, pbuf, dsbuf, plo, dslo, bias, grad, gsend, grecv, *rest,
):
    n_st = len(stages)
    slots = rest[:n_st]
    (small_sem, q_sem, do_sem, own_sem, kv_sem, out_sem, g_rs) = rest[n_st:n_st + 7]
    st_ss = rest[n_st + 7:2 * n_st + 7]
    st_rs = rest[2 * n_st + 7:3 * n_st + 7]
    reply_sem = rest[3 * n_st + 7]
    line_sems = rest[3 * n_st + 8:]
    groups, length, width = q_vm.shape
    per = width // HEAD
    rows = k_hbm.shape[1]
    half = length // 2
    scale = HEAD ** -0.5
    to_exp2 = scale * math.log2(math.e)
    sec = lax.axis_index("section")
    dp = lax.axis_index("dp")

    def sec_peer(off):
        return lax.rem(sec + off, sections)

    strides = []
    stride = 1
    for r in stages:
        strides.append(stride)
        stride *= r

    def member(s):
        return lax.rem(dp // strides[s], stages[s])

    def st_peer(s, off):
        mine = member(s)
        other = lax.rem(mine + off, stages[s])
        return dp + (other - mine) * strides[s]

    near, far = near_split(stages)
    row, seat = (dp // near, lax.rem(dp, near)) if near else (0, 0)

    def dp_signal(sem, when, offset):
        @pl.when(when)
        def _():
            pl.semaphore_signal(sem, inc=1, device_id={"dp": dp + offset}, device_id_type=MESH)

    def signal_up(sem):
        dp_signal(sem, row < far - 1, near)
        for off in range(1, near):
            dp_signal(sem, seat < near - off, off)

    def signal_down(sem):
        dp_signal(sem, row > 0, -near)
        for off in range(1, near):
            dp_signal(sem, seat >= off, -off)

    def line_signal(sem):
        dp_signal(sem, row > 0, -near)
        dp_signal(sem, row < far - 1, near)

    below = jnp.where(row > 0, 1, 0)
    above = jnp.where(row < far - 1, 1, 0)
    barrier = pltpu.get_barrier_semaphore()
    count = 0
    for off in range(1, sections):
        pl.semaphore_signal(barrier, inc=1, device_id={"section": sec_peer(off)}, device_id_type=MESH)
        count += 1
    if near:
        signal_up(barrier)
        count = count + below + seat
    else:
        for s in range(n_st):
            for off in range(1, stages[s]):
                pl.semaphore_signal(barrier, inc=1, device_id={"dp": st_peer(s, off)}, device_id_type=MESH)
                count += 1

    my_rows = pl.ds(pl.multiple_of(sec * rows, rows), rows)

    def hcols(g):
        return pl.ds(pl.multiple_of(g * HEAD, HEAD), HEAD)

    def wcols(g):
        return pl.ds(pl.multiple_of(g * width, HEAD), width)

    def local_in(g):
        return (
            pltpu.make_async_copy(k_hbm.at[0, :, hcols(g)], k_vm.at[g, my_rows, :], own_sem),
            pltpu.make_async_copy(v_hbm.at[0, :, hcols(g)], v_vm.at[g, my_rows, :], own_sem),
            pltpu.make_async_copy(q_hbm.at[0, 0, :, wcols(g)], q_vm.at[g], q_sem),
            pltpu.make_async_copy(do_hbm.at[0, 0, :, wcols(g)], do_vm.at[g], do_sem),
        )

    def kv_copies(g, off):
        made = []
        for src, dst in ((k_hbm, k_vm), (v_hbm, v_vm)):
            made.append(pltpu.make_async_remote_copy(
                src_ref=src.at[0, :, hcols(g)],
                dst_ref=dst.at[g, my_rows, :],
                send_sem=out_sem.at[off - 1],
                recv_sem=kv_sem.at[g],
                device_id={"section": sec_peer(off)},
                device_id_type=MESH,
            ))
        return made

    def grad_copy(g, off):
        peer = sec_peer(off)
        return pltpu.make_async_remote_copy(
            src_ref=gsend.at[g, pl.ds(pl.multiple_of(peer * rows, rows), rows), :],
            dst_ref=grecv.at[off - 1, g],
            send_sem=out_sem.at[off - 1],
            recv_sem=g_rs.at[off - 1],
            device_id={"section": peer},
            device_id_type=MESH,
        )

    def arrival(g):
        return g if n_st > 1 else jnp.where(g == groups - 1, 1, 0)

    def st_copy(s, g, off):
        mine = member(s)
        return pltpu.make_async_remote_copy(
            src_ref=slots[s].at[g, mine],
            dst_ref=slots[s].at[g, mine],
            send_sem=st_ss[s],
            recv_sem=st_rs[s].at[arrival(g)],
            device_id={"dp": st_peer(s, off)},
            device_id_type=MESH,
        )

    def drain(ref, sem):
        pltpu.make_async_copy(ref, ref, sem).wait()

    def slot_sum(s, g):
        total = slots[s][g, 0].astype(F32)
        for m in range(1, stages[s]):
            total = total + slots[s][g, m].astype(F32)
        return total

    def st_total(s, g):
        drain(slots[s].at[g, :stages[s] - 1], st_rs[s].at[g])
        return slot_sum(s, g)

    def st_start(s, g):
        for off in range(1, stages[s]):
            st_copy(s, g, off).start()

    def st_send(s, g, value):
        slots[s][g, member(s)] = value.astype(BF)
        st_start(s, g)

    small = [
        pltpu.make_async_copy(src, dst, small_sem.at[i])
        for i, (src, dst) in enumerate(((doc_hbm, doc_ref), (qs_hbm, qs_ref), (ks_hbm, ks_ref)))
    ]
    for c in small:
        c.start()

    @pl.loop(0, groups)
    def _(g):
        for c in local_in(g):
            c.start()

    pl.semaphore_wait(barrier, count)

    def send_kv(first, last):
        for g in range(first, last):
            for off in range(1, sections):
                for c in kv_copies(g, off):
                    c.start()

    second = lax.rem(dp, 2) == 1
    send_kv(0, 1)

    @pl.when(jnp.logical_not(second))
    def _():
        send_kv(1, groups)

    if near:
        signal_down(reply_sem)

    for c in small:
        c.wait()
    doc = doc_ref[0]
    j_pos = lax.broadcasted_iota(jnp.int32, (length, length), 0)
    i_pos = lax.broadcasted_iota(jnp.int32, (length, length), 1)
    visible = (j_pos <= i_pos) & ((i_pos < doc) | (j_pos >= doc))
    shade = jnp.where(visible, 0.0, -1e30).astype(F32)
    bias[0] = shade[:half, :half]
    bias[1] = shade[:half, half:]
    bias[2] = shade[half:, half:]

    drain(q_vm, q_sem)

    def prepare(g):
        for h in range(per):
            q_f = q_vm[g, :, h * HEAD:(h + 1) * HEAD].astype(F32)
            q_scale = qs_ref[:, pl.ds(pl.multiple_of(g * width + h * HEAD, HEAD), HEAD)]
            qf_vm[g, h] = q_f
            ql_vm[g, h] = (q_f * q_scale).astype(BF)

    pl.loop(0, groups)(prepare)

    @pl.when(second)
    def _():
        send_kv(1, groups)

    if near:
        replies = above + near - 1 - seat

        @pl.when(replies > 0)
        def _():
            pl.semaphore_wait(reply_sem, replies)
    if line_sems:
        line_signal(line_sems[0])

    drain(do_vm, do_sem)
    drain(grecv.at[0], own_sem)

    def weigh(xs, ds):
        top = jnp.max(functools.reduce(jnp.maximum, xs), axis=0, keepdims=True)
        es = [jnp.exp2((x - top) * to_exp2) for x in xs]
        inv = 1.0 / jnp.sum(functools.reduce(jnp.add, es), axis=0, keepdims=True)
        ps = [e * inv for e in es]
        r = [p * d[...] for p, d in zip(ps, ds)]
        r = jnp.sum(functools.reduce(jnp.add, r), axis=0, keepdims=True)
        return [(p.astype(BF), (p * (d[...] - r)).astype(BF)) for p, d in zip(ps, ds)]

    lead = rows >= half

    def ahead(g):
        k_low = (k_vm[g, :half].astype(F32) * ks_ref[:, hcols(g)]).astype(BF)

        def dots(h):
            d_out = do_vm[g, :half, h * HEAD:(h + 1) * HEAD]
            sbuf[h % 2, 0] = lax.dot_general(k_low, ql_vm[g, h, :half], NT, preferred_element_type=F32)
            dbuf[h % 2, 0] = lax.dot_general(v_vm[g, :half], d_out, NT, preferred_element_type=F32)

        dots(0)
        for h in range(per):
            if h + 1 < per:
                dots(h + 1)
            plo[g, h], dslo[g, h] = weigh([sbuf[h % 2, 0] + bias[0]], [dbuf.at[h % 2, 0]])[0]

    if lead:
        @pl.when(sec == 0)
        def _():
            pl.loop(0, groups)(ahead)

    if line_sems:
        pl.semaphore_wait(line_sems[0], below + above)
    if line_sems[1:]:
        line_signal(line_sems[1])
    early = len(line_sems[1:])

    def when(cond):
        if isinstance(cond, bool):
            return lambda f: f() if cond else None
        return pl.when(cond)

    def one_group(g, last, early_lo):
        drain(grecv.at[:, g], kv_sem.at[g])
        k_scale = ks_ref[:, hcols(g)]
        k_low = (k_vm[g].astype(F32) * k_scale).astype(BF)
        k0, k1 = k_low[:half], k_low[half:]
        gain_rows = []

        def d_out_of(h):
            return do_vm[g, :, h * HEAD:(h + 1) * HEAD]

        def scores(h):
            q_low = ql_vm[g, h]
            if early_lo:
                sbuf[h % 2, 1] = lax.dot_general(k0, q_low[half:], NT, preferred_element_type=F32)
            else:
                x = lax.dot_general(k0, q_low, NT, preferred_element_type=F32)
                sbuf[h % 2, 0], sbuf[h % 2, 1] = x[:, :half], x[:, half:]
            sbuf[h % 2, 2] = lax.dot_general(k1, q_low[half:], NT, preferred_element_type=F32)

        def d_probs(h):
            d_out = d_out_of(h)
            if early_lo:
                dbuf[h % 2, 1] = lax.dot_general(v_vm[g, :half], d_out[half:], NT, preferred_element_type=F32)
            else:
                x = lax.dot_general(v_vm[g, :half], d_out, NT, preferred_element_type=F32)
                dbuf[h % 2, 0], dbuf[h % 2, 1] = x[:, :half], x[:, half:]
            dbuf[h % 2, 2] = lax.dot_general(v_vm[g, half:], d_out[half:], NT, preferred_element_type=F32)

        def softmax(h, blocks):
            b = h % 2
            made = weigh([sbuf[b, i] + bias[i] for i in blocks], [dbuf.at[b, i] for i in blocks])
            for i, (p, ds) in zip(blocks, made):
                if i:
                    pbuf[h, i - 1], dsbuf[h, i - 1] = p, ds
                else:
                    plo[g, h], dslo[g, h] = p, ds

        def wide(ref, h):
            first = plo if ref is pbuf else dslo
            return jnp.concatenate([first[g, h], ref[h, 0]], axis=1)

        def add(h, rows_, cols_, x):
            if h == 0:
                grad[g, rows_, cols_] = x
            else:
                grad[g, rows_, cols_] += x

        lo, hi = slice(0, half), slice(half, 2 * half)
        kc, vc = slice(0, HEAD), slice(HEAD, 2 * HEAD)

        def kv_grads(h):
            d_out, q_low = d_out_of(h), ql_vm[g, h]
            add(h, lo, vc, jnp.dot(wide(pbuf, h), d_out, preferred_element_type=F32))
            add(h, hi, vc, jnp.dot(pbuf[h, 1], d_out[half:], preferred_element_type=F32))
            add(h, lo, kc, jnp.dot(wide(dsbuf, h), q_low, preferred_element_type=F32))
            add(h, hi, kc, jnp.dot(dsbuf[h, 1], q_low[half:], preferred_element_type=F32))

        def q_grads(h):
            cols = pl.ds(pl.multiple_of(g * width + h * HEAD, HEAD), HEAD)
            hi_ds = jnp.concatenate([dsbuf[h, 0], dsbuf[h, 1]], axis=0)
            dq = jnp.concatenate([
                lax.dot_general(dslo[g, h], k_low[:half], (((0,), (0,)), ((), ())), preferred_element_type=F32),
                lax.dot_general(hi_ds, k_low, (((0,), (0,)), ((), ())), preferred_element_type=F32),
            ], axis=0)
            dq_ref[0, 0, :, cols] = (dq * (qs_ref[:, cols] * scale)).astype(BF)
            gain_rows.append(jnp.sum(dq * qf_vm[g, h], axis=0, keepdims=True))

        def all_kv_grads():
            heads = range(per)
            for ref, right, cols in (
                (pbuf, [d_out_of(h) for h in heads], vc),
                (dsbuf, [ql_vm[g, h] for h in heads], kc),
            ):
                grad[g, lo, cols] = jnp.dot(
                    jnp.concatenate([wide(ref, h) for h in heads], axis=1),
                    jnp.concatenate(right, axis=0), preferred_element_type=F32,
                )
                grad[g, hi, cols] = jnp.dot(
                    jnp.concatenate([ref[h, 1] for h in heads], axis=1),
                    jnp.concatenate([x[half:] for x in right], axis=0), preferred_element_type=F32,
                )

        def start_grad(e):
            for off in range(1, sections):
                grad_copy(e, off).start()

        def send_grads():
            key_term = grad[g, :, kc] * (k_scale * scale)
            grad[g, :, kc] = key_term
            gsend[g, :, kc] = key_term.astype(BF)
            gsend[g, :, vc] = grad[g, :, vc].astype(BF)
            if last:
                start_grad(g)
                return

            @when(g == groups - 2)
            def _():
                for e in range(groups - 1):
                    start_grad(e)

        def send_gains():
            spare = slots[0].shape[2] - per
            rows_ = gain_rows + ([jnp.zeros((spare, HEAD), F32)] if spare else [])
            slots[0][g, member(0)] = jnp.concatenate(rows_, axis=0).astype(BF)
            for i in range(early):
                @when(g == i)
                def _():
                    pl.semaphore_wait(line_sems[i + 1], below + above)
                    if i + 1 < early:
                        line_signal(line_sems[i + 2])
            hold = max(early - 1, 0)

            @when(g == hold)
            def _():
                for e in range(hold):
                    st_start(0, e)

            @when(g >= hold)
            def _():
                st_start(0, g)

        scores(0)
        d_probs(0)
        for h in range(per):
            if h + 1 < per:
                scores(h + 1)
            if not early_lo:
                softmax(h, (0,))
            if h + 1 < per:
                d_probs(h + 1)
            if h and not last:
                kv_grads(h - 1)
            softmax(h, (1, 2))
            if h > 1 and not last:
                q_grads(h - 2)
            if h and last:
                q_grads(h - 1)
        if last:
            q_grads(per - 1)
            send_gains()
            all_kv_grads()
            send_grads()
        else:
            if per > 1:
                q_grads(per - 2)
            kv_grads(per - 1)
            q_grads(per - 1)
            send_grads()
            send_gains()

        for s in range(1, n_st):
            @when(g >= LAG * s)
            def _():
                st_send(s, g - LAG * s, st_total(s - 1, g - LAG * s))

    def all_groups(early_lo):
        pl.loop(0, groups - 1)(lambda g: one_group(g, False, early_lo))
        one_group(groups - 1, True, early_lo)

    if lead:
        @pl.when(sec == 0)
        def _():
            all_groups(True)

        @pl.when(sec != 0)
        def _():
            all_groups(False)
    else:
        all_groups(False)

    def finish_gain(g, total):
        total = total * (scale / replicas)
        key_sum = 0.0
        for h in range(per):
            cols = slice((g * per + h) * HEAD, (g * per + h + 1) * HEAD)
            qgain_ref[:, cols] = total[h:h + 1]
            key_sum = key_sum + total[h:h + 1] * qs_ref[:, cols]
        cols = slice(g * HEAD, (g + 1) * HEAD)
        kgain_ref[:, cols] = key_sum / ks_ref[:, cols]

    def finish_grad(g):
        total = grad[g, my_rows, :]
        for off in range(1, sections):
            total = total + grecv[off - 1, g].astype(F32)
        kg_ref[0, :, g * HEAD:(g + 1) * HEAD] = total[:, :HEAD].astype(BF)
        vg_ref[0, :, g * HEAD:(g + 1) * HEAD] = total[:, HEAD:].astype(BF)

    for t in range(groups, groups + LAG * (n_st - 1)):
        for s in range(n_st - 1, 0, -1):
            g = t - LAG * s
            if 0 <= g < groups:
                st_send(s, g, st_total(s - 1, g))
    if n_st == 1 and groups > 1:
        drain(slots[0].at[:groups - 1, :stages[0] - 1], st_rs[0].at[0])
        for g in range(groups - 1):
            finish_gain(g, slot_sum(0, g))
    for off in range(1, sections):
        drain(grecv.at[off - 1], g_rs.at[off - 1])
    for g in range(groups):
        finish_grad(g)
    for off in range(1, sections):
        drain(gsend.at[:, :2 * rows], out_sem.at[off - 1])
    if n_st == 1:
        drain(slots[0].at[0, :stages[0] - 1], st_rs[0].at[1])
        finish_gain(groups - 1, slot_sum(0, groups - 1))
    else:
        for g in range(groups):
            finish_gain(g, st_total(n_st - 1, g))

    for s in range(n_st):
        drain(slots[s].at[:, :stages[s] - 1], st_ss[s])


def write_out(*refs):
    n = len(refs) // 2
    sems = refs[-1]
    copies = [pltpu.make_async_copy(refs[i], refs[n + i], sems.at[i]) for i in range(n)]
    for c in copies:
        c.start()
    for c in copies:
        c.wait()


def solution(mesh):
    sections = mesh.shape["section"]
    replicas = mesh.shape["dp"]
    stages = radices(replicas)
    n_st = len(stages)

    def on_device(queries, keys, values, query_gain, key_channel_scale, out_grad, doc_start):
        length = queries.shape[2]
        rows, kv_width = keys.shape[1], keys.shape[2]
        groups, half = kv_width // HEAD, length // 2
        width = queries.shape[3] // groups
        per = width // HEAD
        gain_rows = -(-per // 8) * 8
        vmem = pl.BlockSpec(memory_space=pltpu.VMEM)
        hbm = pl.BlockSpec(memory_space=pl.ANY)
        dma = pltpu.SemaphoreType.DMA
        peers = sections - 1
        scratch = [
            pltpu.SMEM(doc_start.shape, jnp.int32),
            pltpu.VMEM(query_gain.shape, F32),
            pltpu.VMEM(key_channel_scale.shape, F32),
            pltpu.VMEM((groups, length, width), BF),
            pltpu.VMEM((groups, length, width), BF),
            pltpu.VMEM((groups, length, HEAD), BF),
            pltpu.VMEM((groups, length, HEAD), BF),
            pltpu.VMEM((groups, width // HEAD, length, HEAD), BF),
            pltpu.VMEM((groups, width // HEAD, length, HEAD), F32),
            pltpu.VMEM((2, 3, half, half), F32),
            pltpu.VMEM((2, 3, half, half), F32),
            pltpu.VMEM((per, 2, half, half), BF),
            pltpu.VMEM((per, 2, half, half), BF),
            pltpu.VMEM((groups, per, half, half), BF),
            pltpu.VMEM((groups, per, half, half), BF),
            pltpu.VMEM((3, half, half), F32),
            pltpu.VMEM((groups, length, 2 * HEAD), F32),
            pltpu.VMEM((groups, length, 2 * HEAD), BF),
            pltpu.VMEM((peers, groups, rows, 2 * HEAD), BF),
        ]
        scratch += [pltpu.VMEM((groups, r, gain_rows, HEAD), BF) for r in stages]
        scratch += [dma((3,)), dma, dma, dma, dma((groups,)), dma((peers,)), dma((peers,))]
        scratch += [dma] * n_st + [dma((groups if n_st > 1 else 2,))] * n_st
        scratch += [pltpu.SemaphoreType.REGULAR] * max(near_split(stages)[1], 1)
        shapes = (
            jax.ShapeDtypeStruct(queries.shape, BF),
            jax.ShapeDtypeStruct(keys.shape, BF),
            jax.ShapeDtypeStruct(values.shape, BF),
            jax.ShapeDtypeStruct(query_gain.shape, F32),
            jax.ShapeDtypeStruct(key_channel_scale.shape, F32),
        )
        held = pl.pallas_call(
            functools.partial(kernel, sections, replicas, stages),
            out_shape=tuple(pltpu.VMEM(x.shape, x.dtype) for x in shapes),
            in_specs=[pl.BlockSpec(memory_space=pltpu.HBM)] + [hbm] * 6,
            out_specs=(vmem,) * 5,
            scratch_shapes=scratch,
            compiler_params=pltpu.CompilerParams(collective_id=0, has_side_effects=True),
        )(doc_start, queries, keys, values, query_gain, key_channel_scale, out_grad)
        return pl.pallas_call(
            write_out,
            out_shape=shapes,
            in_specs=[vmem] * 5,
            out_specs=(hbm,) * 5,
            scratch_shapes=[dma((5,))],
        )(*[pltpu.with_memory_space_constraint(x, pltpu.VMEM) for x in held])

    in_specs = (
        P("section", "dp", None, None),
        P("dp", "section", None),
        P("dp", "section", None),
        P("section", None),
        P("section", None),
        P("section", "dp", None, None),
        P("dp"),
    )
    out_specs = (
        P("section", "dp", None, None),
        P("dp", "section", None),
        P("dp", "section", None),
        P("section", None),
        P("section", None),
    )
    return jax.shard_map(
        on_device, mesh=mesh, in_specs=in_specs, out_specs=out_specs, check_vma=False
    )
```

```python
import functools
import math

import jax
import jax.numpy as jnp
from jax import lax
from jax.experimental import pallas as pl
from jax.experimental.pallas import tpu as pltpu
from jax.sharding import PartitionSpec as P

HEAD = 128
LAG = 2
DIRECT = 16
NEAR = 4
MESH = pl.DeviceIdType.MESH
BF = jnp.bfloat16
F32 = jnp.float32
NT = (((1,), (1,)), ((), ()))


def radices(n):
    out = []
    while n > 1:
        r = next((r for r in range(DIRECT, 1, -1) if n % r == 0), n)
        out.append(r)
        n //= r
    return out


def near_split(stages):
    if len(stages) == 1 and stages[0] % NEAR == 0:
        return NEAR, stages[0] // NEAR
    return 0, 0


def kernel(
    sections, replicas, stages,
    doc_hbm, q_hbm, k_hbm, v_hbm, qs_hbm, ks_hbm, do_hbm,
    dq_ref, kg_ref, vg_ref, qgain_ref, kgain_ref,
    doc_ref, qs_ref, ks_ref, q_vm, do_vm, k_vm, v_vm, ql_vm, qf_vm, sbuf, dbuf, pbuf, dsbuf, plo, dslo, bias, grad, gsend, grecv, *rest,
):
    n_st = len(stages)
    slots = rest[:n_st]
    (small_sem, q_sem, do_sem, own_sem, kv_sem, out_sem, g_rs) = rest[n_st:n_st + 7]
    st_ss = rest[n_st + 7:2 * n_st + 7]
    st_rs = rest[2 * n_st + 7:3 * n_st + 7]
    reply_sem = rest[3 * n_st + 7]
    line_sems = rest[3 * n_st + 8:]
    groups, length, width = q_vm.shape
    per = width // HEAD
    rows = k_hbm.shape[1]
    half = length // 2
    scale = HEAD ** -0.5
    to_exp2 = scale * math.log2(math.e)
    sec = lax.axis_index("section")
    dp = lax.axis_index("dp")

    def sec_peer(off):
        return lax.rem(sec + off, sections)

    strides = []
    stride = 1
    for r in stages:
        strides.append(stride)
        stride *= r

    def member(s):
        return lax.rem(dp // strides[s], stages[s])

    def st_peer(s, off):
        mine = member(s)
        other = lax.rem(mine + off, stages[s])
        return dp + (other - mine) * strides[s]

    near, far = near_split(stages)
    row, seat = (dp // near, lax.rem(dp, near)) if near else (0, 0)

    def dp_signal(sem, when, offset):
        @pl.when(when)
        def _():
            pl.semaphore_signal(sem, inc=1, device_id={"dp": dp + offset}, device_id_type=MESH)

    def signal_up(sem):
        dp_signal(sem, row < far - 1, near)
        for off in range(1, near):
            dp_signal(sem, seat < near - off, off)

    def signal_down(sem):
        dp_signal(sem, row > 0, -near)
        for off in range(1, near):
            dp_signal(sem, seat >= off, -off)

    def line_signal(sem):
        dp_signal(sem, row > 0, -near)
        dp_signal(sem, row < far - 1, near)

    below = jnp.where(row > 0, 1, 0)
    above = jnp.where(row < far - 1, 1, 0)
    barrier = pltpu.get_barrier_semaphore()
    count = 0
    for off in range(1, sections):
        pl.semaphore_signal(barrier, inc=1, device_id={"section": sec_peer(off)}, device_id_type=MESH)
        count += 1
    if near:
        signal_up(barrier)
        count = count + below + seat
    else:
        for s in range(n_st):
            for off in range(1, stages[s]):
                pl.semaphore_signal(barrier, inc=1, device_id={"dp": st_peer(s, off)}, device_id_type=MESH)
                count += 1

    my_rows = pl.ds(pl.multiple_of(sec * rows, rows), rows)

    def hcols(g):
        return pl.ds(pl.multiple_of(g * HEAD, HEAD), HEAD)

    def wcols(g):
        return pl.ds(pl.multiple_of(g * width, HEAD), width)

    def local_in(g):
        return (
            pltpu.make_async_copy(k_hbm.at[0, :, hcols(g)], k_vm.at[g, my_rows, :], own_sem),
            pltpu.make_async_copy(v_hbm.at[0, :, hcols(g)], v_vm.at[g, my_rows, :], own_sem),
            pltpu.make_async_copy(q_hbm.at[0, 0, :, wcols(g)], q_vm.at[g], q_sem),
            pltpu.make_async_copy(do_hbm.at[0, 0, :, wcols(g)], do_vm.at[g], do_sem),
        )

    def kv_copies(g, off):
        made = []
        for src, dst in ((k_hbm, k_vm), (v_hbm, v_vm)):
            made.append(pltpu.make_async_remote_copy(
                src_ref=src.at[0, :, hcols(g)],
                dst_ref=dst.at[g, my_rows, :],
                send_sem=out_sem.at[off - 1],
                recv_sem=kv_sem.at[g],
                device_id={"section": sec_peer(off)},
                device_id_type=MESH,
            ))
        return made

    def grad_copy(g, off):
        peer = sec_peer(off)
        return pltpu.make_async_remote_copy(
            src_ref=gsend.at[g, pl.ds(pl.multiple_of(peer * rows, rows), rows), :],
            dst_ref=grecv.at[off - 1, g],
            send_sem=out_sem.at[off - 1],
            recv_sem=g_rs.at[off - 1],
            device_id={"section": peer},
            device_id_type=MESH,
        )

    def arrival(g):
        return g if n_st > 1 else jnp.where(g == groups - 1, 1, 0)

    def st_copy(s, g, off):
        mine = member(s)
        return pltpu.make_async_remote_copy(
            src_ref=slots[s].at[g, mine],
            dst_ref=slots[s].at[g, mine],
            send_sem=st_ss[s],
            recv_sem=st_rs[s].at[arrival(g)],
            device_id={"dp": st_peer(s, off)},
            device_id_type=MESH,
        )

    def drain(ref, sem):
        pltpu.make_async_copy(ref, ref, sem).wait()

    def slot_sum(s, g):
        total = slots[s][g, 0].astype(F32)
        for m in range(1, stages[s]):
            total = total + slots[s][g, m].astype(F32)
        return total

    def st_total(s, g):
        drain(slots[s].at[g, :stages[s] - 1], st_rs[s].at[g])
        return slot_sum(s, g)

    def st_start(s, g):
        for off in range(1, stages[s]):
            st_copy(s, g, off).start()

    def st_send(s, g, value):
        slots[s][g, member(s)] = value.astype(BF)
        st_start(s, g)

    small = [
        pltpu.make_async_copy(src, dst, small_sem.at[i])
        for i, (src, dst) in enumerate(((doc_hbm, doc_ref), (qs_hbm, qs_ref), (ks_hbm, ks_ref)))
    ]
    for c in small:
        c.start()

    @pl.loop(0, groups)
    def _(g):
        for c in local_in(g):
            c.start()

    pl.semaphore_wait(barrier, count)

    def send_kv(first, last):
        for g in range(first, last):
            for off in range(1, sections):
                for c in kv_copies(g, off):
                    c.start()

    second = lax.rem(dp, 2) == 1
    send_kv(0, 1)

    @pl.when(jnp.logical_not(second))
    def _():
        send_kv(1, groups)

    if near:
        signal_down(reply_sem)

    for c in small:
        c.wait()
    doc = doc_ref[0]
    j_pos = lax.broadcasted_iota(jnp.int32, (length, length), 0)
    i_pos = lax.broadcasted_iota(jnp.int32, (length, length), 1)
    visible = (j_pos <= i_pos) & ((i_pos < doc) | (j_pos >= doc))
    shade = jnp.where(visible, 0.0, -1e30).astype(F32)
    bias[0] = shade[:half, :half]
    bias[1] = shade[:half, half:]
    bias[2] = shade[half:, half:]

    drain(q_vm, q_sem)

    def prepare(g):
        for h in range(per):
            q_f = q_vm[g, :, h * HEAD:(h + 1) * HEAD].astype(F32)
            q_scale = qs_ref[:, pl.ds(pl.multiple_of(g * width + h * HEAD, HEAD), HEAD)]
            qf_vm[g, h] = q_f
            ql_vm[g, h] = (q_f * q_scale).astype(BF)

    pl.loop(0, groups)(prepare)

    @pl.when(second)
    def _():
        send_kv(1, groups)

    drain(do_vm, do_sem)
    drain(grecv.at[0], own_sem)

    def weigh(xs, ds):
        top = jnp.max(functools.reduce(jnp.maximum, xs), axis=0, keepdims=True)
        es = [jnp.exp2((x - top) * to_exp2) for x in xs]
        inv = 1.0 / jnp.sum(functools.reduce(jnp.add, es), axis=0, keepdims=True)
        ps = [e * inv for e in es]
        r = [p * d[...] for p, d in zip(ps, ds)]
        r = jnp.sum(functools.reduce(jnp.add, r), axis=0, keepdims=True)
        return [(p.astype(BF), (p * (d[...] - r)).astype(BF)) for p, d in zip(ps, ds)]

    lead = rows >= half

    def ahead(g):
        k_low = (k_vm[g, :half].astype(F32) * ks_ref[:, hcols(g)]).astype(BF)

        def dots(h):
            d_out = do_vm[g, :half, h * HEAD:(h + 1) * HEAD]
            sbuf[h % 2, 0] = lax.dot_general(k_low, ql_vm[g, h, :half], NT, preferred_element_type=F32)
            dbuf[h % 2, 0] = lax.dot_general(v_vm[g, :half], d_out, NT, preferred_element_type=F32)

        dots(0)
        for h in range(per):
            if h + 1 < per:
                dots(h + 1)
            plo[g, h], dslo[g, h] = weigh([sbuf[h % 2, 0] + bias[0]], [dbuf.at[h % 2, 0]])[0]

    if lead:
        @pl.when(sec == 0)
        def _():
            pl.loop(0, groups // 2)(ahead)

    if near:
        replies = above + near - 1 - seat

        @pl.when(replies > 0)
        def _():
            pl.semaphore_wait(reply_sem, replies)
    if line_sems:
        line_signal(line_sems[0])

    if lead:
        @pl.when(sec == 0)
        def _():
            pl.loop(groups // 2, groups)(ahead)

    if line_sems:
        pl.semaphore_wait(line_sems[0], below + above)
    if line_sems[1:]:
        line_signal(line_sems[1])
    early = len(line_sems[1:])

    def when(cond):
        if isinstance(cond, bool):
            return lambda f: f() if cond else None
        return pl.when(cond)

    def one_group(g, last, early_lo):
        drain(grecv.at[:, g], kv_sem.at[g])
        k_scale = ks_ref[:, hcols(g)]
        k_low = (k_vm[g].astype(F32) * k_scale).astype(BF)
        k0, k1 = k_low[:half], k_low[half:]
        gain_rows = []

        def d_out_of(h):
            return do_vm[g, :, h * HEAD:(h + 1) * HEAD]

        def scores(h):
            q_low = ql_vm[g, h]
            if early_lo:
                sbuf[h % 2, 1] = lax.dot_general(k0, q_low[half:], NT, preferred_element_type=F32)
            else:
                x = lax.dot_general(k0, q_low, NT, preferred_element_type=F32)
                sbuf[h % 2, 0], sbuf[h % 2, 1] = x[:, :half], x[:, half:]
            sbuf[h % 2, 2] = lax.dot_general(k1, q_low[half:], NT, preferred_element_type=F32)

        def d_probs(h):
            d_out = d_out_of(h)
            if early_lo:
                dbuf[h % 2, 1] = lax.dot_general(v_vm[g, :half], d_out[half:], NT, preferred_element_type=F32)
            else:
                x = lax.dot_general(v_vm[g, :half], d_out, NT, preferred_element_type=F32)
                dbuf[h % 2, 0], dbuf[h % 2, 1] = x[:, :half], x[:, half:]
            dbuf[h % 2, 2] = lax.dot_general(v_vm[g, half:], d_out[half:], NT, preferred_element_type=F32)

        def softmax(h, blocks):
            b = h % 2
            made = weigh([sbuf[b, i] + bias[i] for i in blocks], [dbuf.at[b, i] for i in blocks])
            for i, (p, ds) in zip(blocks, made):
                if i:
                    pbuf[h, i - 1], dsbuf[h, i - 1] = p, ds
                else:
                    plo[g, h], dslo[g, h] = p, ds

        def wide(ref, h):
            first = plo if ref is pbuf else dslo
            return jnp.concatenate([first[g, h], ref[h, 0]], axis=1)

        def add(h, rows_, cols_, x):
            if h == 0:
                grad[g, rows_, cols_] = x
            else:
                grad[g, rows_, cols_] += x

        lo, hi = slice(0, half), slice(half, 2 * half)
        kc, vc = slice(0, HEAD), slice(HEAD, 2 * HEAD)

        def kv_grads(h):
            d_out, q_low = d_out_of(h), ql_vm[g, h]
            add(h, lo, vc, jnp.dot(wide(pbuf, h), d_out, preferred_element_type=F32))
            add(h, hi, vc, jnp.dot(pbuf[h, 1], d_out[half:], preferred_element_type=F32))
            add(h, lo, kc, jnp.dot(wide(dsbuf, h), q_low, preferred_element_type=F32))
            add(h, hi, kc, jnp.dot(dsbuf[h, 1], q_low[half:], preferred_element_type=F32))

        def q_grads(h):
            cols = pl.ds(pl.multiple_of(g * width + h * HEAD, HEAD), HEAD)
            hi_ds = jnp.concatenate([dsbuf[h, 0], dsbuf[h, 1]], axis=0)
            dq = jnp.concatenate([
                lax.dot_general(dslo[g, h], k_low[:half], (((0,), (0,)), ((), ())), preferred_element_type=F32),
                lax.dot_general(hi_ds, k_low, (((0,), (0,)), ((), ())), preferred_element_type=F32),
            ], axis=0)
            dq_ref[0, 0, :, cols] = (dq * (qs_ref[:, cols] * scale)).astype(BF)
            gain_rows.append(jnp.sum(dq * qf_vm[g, h], axis=0, keepdims=True))

        def all_kv_grads():
            heads = range(per)
            for ref, right, cols in (
                (pbuf, [d_out_of(h) for h in heads], vc),
                (dsbuf, [ql_vm[g, h] for h in heads], kc),
            ):
                grad[g, lo, cols] = jnp.dot(
                    jnp.concatenate([wide(ref, h) for h in heads], axis=1),
                    jnp.concatenate(right, axis=0), preferred_element_type=F32,
                )
                grad[g, hi, cols] = jnp.dot(
                    jnp.concatenate([ref[h, 1] for h in heads], axis=1),
                    jnp.concatenate([x[half:] for x in right], axis=0), preferred_element_type=F32,
                )

        def start_grad(e):
            for off in range(1, sections):
                grad_copy(e, off).start()

        def send_grads():
            key_term = grad[g, :, kc] * (k_scale * scale)
            grad[g, :, kc] = key_term
            gsend[g, :, kc] = key_term.astype(BF)
            gsend[g, :, vc] = grad[g, :, vc].astype(BF)
            if last:
                start_grad(g)
                return

            @when(g == groups - 2)
            def _():
                for e in range(groups - 1):
                    start_grad(e)

        def send_gains():
            spare = slots[0].shape[2] - per
            rows_ = gain_rows + ([jnp.zeros((spare, HEAD), F32)] if spare else [])
            slots[0][g, member(0)] = jnp.concatenate(rows_, axis=0).astype(BF)
            for i in range(early):
                @when(g == i)
                def _():
                    pl.semaphore_wait(line_sems[i + 1], below + above)
                    if i + 1 < early:
                        line_signal(line_sems[i + 2])
            hold = max(early - 1, 0)

            @when(g == hold)
            def _():
                for e in range(hold):
                    st_start(0, e)

            @when(g >= hold)
            def _():
                st_start(0, g)

        scores(0)
        d_probs(0)
        for h in range(per):
            if h + 1 < per:
                scores(h + 1)
            if not early_lo:
                softmax(h, (0,))
            if h + 1 < per:
                d_probs(h + 1)
            if h > 1 or (h and not last):
                kv_grads(h - 1 - int(last))
            softmax(h, (1, 2))
            if h > 1:
                q_grads(h - 2)
        if last:
            if per > 1:
                q_grads(per - 2)
            q_grads(per - 1)
            send_gains()
            kv_grads(per - 2)
            kv_grads(per - 1)
            send_grads()
        else:
            if per > 1:
                q_grads(per - 2)
            kv_grads(per - 1)
            q_grads(per - 1)
            send_grads()
            send_gains()

        for s in range(1, n_st):
            @when(g >= LAG * s)
            def _():
                st_send(s, g - LAG * s, st_total(s - 1, g - LAG * s))

    def all_groups(early_lo):
        pl.loop(0, groups - 1)(lambda g: one_group(g, False, early_lo))
        one_group(groups - 1, True, early_lo)

    if lead:
        @pl.when(sec == 0)
        def _():
            all_groups(True)

        @pl.when(sec != 0)
        def _():
            all_groups(False)
    else:
        all_groups(False)

    def finish_gain(g, total):
        total = total * (scale / replicas)
        key_sum = 0.0
        for h in range(per):
            cols = slice((g * per + h) * HEAD, (g * per + h + 1) * HEAD)
            qgain_ref[:, cols] = total[h:h + 1]
            key_sum = key_sum + total[h:h + 1] * qs_ref[:, cols]
        cols = slice(g * HEAD, (g + 1) * HEAD)
        kgain_ref[:, cols] = key_sum / ks_ref[:, cols]

    def finish_grad(g):
        total = grad[g, my_rows, :]
        for off in range(1, sections):
            total = total + grecv[off - 1, g].astype(F32)
        kg_ref[0, :, g * HEAD:(g + 1) * HEAD] = total[:, :HEAD].astype(BF)
        vg_ref[0, :, g * HEAD:(g + 1) * HEAD] = total[:, HEAD:].astype(BF)

    for t in range(groups, groups + LAG * (n_st - 1)):
        for s in range(n_st - 1, 0, -1):
            g = t - LAG * s
            if 0 <= g < groups:
                st_send(s, g, st_total(s - 1, g))
    if n_st == 1 and groups > 1:
        drain(slots[0].at[:groups - 1, :stages[0] - 1], st_rs[0].at[0])
        for g in range(groups - 1):
            finish_gain(g, slot_sum(0, g))
    for off in range(1, sections):
        drain(grecv.at[off - 1], g_rs.at[off - 1])
    for g in range(groups):
        finish_grad(g)
    for off in range(1, sections):
        drain(gsend.at[:, :2 * rows], out_sem.at[off - 1])
    if n_st == 1:
        drain(slots[0].at[0, :stages[0] - 1], st_rs[0].at[1])
        finish_gain(groups - 1, slot_sum(0, groups - 1))
    else:
        for g in range(groups):
            finish_gain(g, st_total(n_st - 1, g))

    for s in range(n_st):
        drain(slots[s].at[:, :stages[s] - 1], st_ss[s])


def write_out(*refs):
    n = len(refs) // 2
    sems = refs[-1]
    copies = [pltpu.make_async_copy(refs[i], refs[n + i], sems.at[i]) for i in range(n)]
    for c in copies:
        c.start()
    for c in copies:
        c.wait()


def solution(mesh):
    sections = mesh.shape["section"]
    replicas = mesh.shape["dp"]
    stages = radices(replicas)
    n_st = len(stages)

    def on_device(queries, keys, values, query_gain, key_channel_scale, out_grad, doc_start):
        length = queries.shape[2]
        rows, kv_width = keys.shape[1], keys.shape[2]
        groups, half = kv_width // HEAD, length // 2
        width = queries.shape[3] // groups
        per = width // HEAD
        gain_rows = -(-per // 8) * 8
        vmem = pl.BlockSpec(memory_space=pltpu.VMEM)
        hbm = pl.BlockSpec(memory_space=pl.ANY)
        dma = pltpu.SemaphoreType.DMA
        peers = sections - 1
        scratch = [
            pltpu.SMEM(doc_start.shape, jnp.int32),
            pltpu.VMEM(query_gain.shape, F32),
            pltpu.VMEM(key_channel_scale.shape, F32),
            pltpu.VMEM((groups, length, width), BF),
            pltpu.VMEM((groups, length, width), BF),
            pltpu.VMEM((groups, length, HEAD), BF),
            pltpu.VMEM((groups, length, HEAD), BF),
            pltpu.VMEM((groups, width // HEAD, length, HEAD), BF),
            pltpu.VMEM((groups, width // HEAD, length, HEAD), F32),
            pltpu.VMEM((2, 3, half, half), F32),
            pltpu.VMEM((2, 3, half, half), F32),
            pltpu.VMEM((per, 2, half, half), BF),
            pltpu.VMEM((per, 2, half, half), BF),
            pltpu.VMEM((groups, per, half, half), BF),
            pltpu.VMEM((groups, per, half, half), BF),
            pltpu.VMEM((3, half, half), F32),
            pltpu.VMEM((groups, length, 2 * HEAD), F32),
            pltpu.VMEM((groups, length, 2 * HEAD), BF),
            pltpu.VMEM((peers, groups, rows, 2 * HEAD), BF),
        ]
        scratch += [pltpu.VMEM((groups, r, gain_rows, HEAD), BF) for r in stages]
        scratch += [dma((3,)), dma, dma, dma, dma((groups,)), dma((peers,)), dma((peers,))]
        scratch += [dma] * n_st + [dma((groups if n_st > 1 else 2,))] * n_st
        scratch += [pltpu.SemaphoreType.REGULAR] * max(near_split(stages)[1], 1)
        shapes = (
            jax.ShapeDtypeStruct(queries.shape, BF),
            jax.ShapeDtypeStruct(keys.shape, BF),
            jax.ShapeDtypeStruct(values.shape, BF),
            jax.ShapeDtypeStruct(query_gain.shape, F32),
            jax.ShapeDtypeStruct(key_channel_scale.shape, F32),
        )
        held = pl.pallas_call(
            functools.partial(kernel, sections, replicas, stages),
            out_shape=tuple(pltpu.VMEM(x.shape, x.dtype) for x in shapes),
            in_specs=[pl.BlockSpec(memory_space=pltpu.HBM)] + [hbm] * 6,
            out_specs=(vmem,) * 5,
            scratch_shapes=scratch,
            compiler_params=pltpu.CompilerParams(collective_id=0, has_side_effects=True),
        )(doc_start, queries, keys, values, query_gain, key_channel_scale, out_grad)
        return pl.pallas_call(
            write_out,
            out_shape=shapes,
            in_specs=[vmem] * 5,
            out_specs=(hbm,) * 5,
            scratch_shapes=[dma((5,))],
        )(*[pltpu.with_memory_space_constraint(x, pltpu.VMEM) for x in held])

    in_specs = (
        P("section", "dp", None, None),
        P("dp", "section", None),
        P("dp", "section", None),
        P("section", None),
        P("section", None),
        P("section", "dp", None, None),
        P("dp"),
    )
    out_specs = (
        P("section", "dp", None, None),
        P("dp", "section", None),
        P("dp", "section", None),
        P("section", None),
        P("section", None),
    )
    return jax.shard_map(
        on_device, mesh=mesh, in_specs=in_specs, out_specs=out_specs, check_vma=False
    )
```
